32 devices in a mesh: seq: 4 (over z), fsdp: 8 (over y, x, core).
Axes of the slice: x: 2, y: 2, z: 4, core: 2. Of those that a mesh axis runs over, the one named last changes fastest.
Arguments:
- tokens: bfloat16 [8, 512, 768], P('fsdp', 'seq'), may hold values from -6 to 6
- positions: int32 [8, 512], P('fsdp', 'seq'), may hold values from 0 to 5117, as said below
- norm1_gain: bfloat16 [768], P('fsdp'), may hold values from 0.5 to 1.5
- qkv_weight: bfloat16 [768, 2304], P('fsdp'), may hold values from -0.57735027 to 0.57735027, as said below
- out_weight: bfloat16 [768, 768], P('fsdp'), may hold values from -6 to 6
- norm2_gain: bfloat16 [768], P('fsdp'), may hold values from 0.5 to 1.5
- in_weight: bfloat16 [768, 2304], P('fsdp'), may hold values from -0.21875 to 0.21875
- down_weight: bfloat16 [1152, 768], P(None, 'fsdp'), may hold values from -0.1875 to 0.1875
- cotangent: bfloat16 [8, 512, 768], P('fsdp', 'seq'), may hold values from -6 to 6
Outputs:
- block_out: bfloat16 [8, 512, 768], P('fsdp', 'seq')
- input_grad: bfloat16 [8, 512, 768], P('fsdp', 'seq')
- qkv_weight_grad: float32 [768, 2304], P('fsdp')
- out_weight_grad: float32 [768, 768], P('fsdp')
- in_weight_grad: float32 [768, 2304], P('fsdp')
- down_weight_grad: float32 [1152, 768], P(None, 'fsdp')
- norm1_gain_grad: float32 [768], P('fsdp')
- norm2_gain_grad: float32 [768], P('fsdp')
The draws below stay inside these ranges and needn't reach their ends.
Inputs may be any that keep to these rules, and one draw needn't show every extreme that they name: Along each sequence the positions rise by 1 or 2 from one token to the next. `qkv_weight`: A projection matrix; every entry lies within 16 / sqrt(768) of zero.
All inputs are finite; a program needn't handle non-finite values.
Results may differ from the reference program's by a relative error of at most 0.019.
Values may be sent and summed in bfloat16 or wider, within the bound.
A program may use at most 128 MiB of HBM per device.

```python
import jax
import jax.numpy as jnp
from jax import lax

D = 768
HEADS = 12
HEAD_DIM = 64
FF = 1152
LEN = 512
SEQS = 8


def draw_positions(key, part):
    offsets = jax.random.randint(jax.random.fold_in(key, 11), (SEQS, 1), 0, 4096)
    strides = jax.random.randint(jax.random.fold_in(key, 12), (SEQS, LEN), 1, 3)
    row_index = jnp.arange(SEQS, dtype=jnp.int32)[:, None]
    offsets = jnp.where(row_index == 0, 0, offsets)
    offsets = jnp.where(row_index == SEQS - 1, 4095, offsets)
    strides = jnp.where(row_index == SEQS - 1, 2, strides)
    rising = jnp.cumsum(strides, axis=1) - strides[:, :1]
    return (offsets + rising).astype(jnp.int32)


def draw_qkv_weight(key, part):
    base = jnp.clip(jax.random.normal(jax.random.fold_in(key, 21), (D, 3 * D), jnp.float32), -4.0, 4.0) * D ** (-0.5)
    return base.astype(jnp.bfloat16)


def block_scale(key, dims, pieces, smallest, largest):
    loudness = 1.0
    for dim, shards_of in pieces:
        heights = jax.random.uniform(jax.random.fold_in(jax.random.fold_in(key, 6), dim), (shards_of,), jnp.float32, smallest / len(pieces), largest / len(pieces))
        loudness = loudness * jnp.repeat(jnp.exp(heights), dims[dim] // shards_of).reshape((-1,) + (1,) * (len(dims) - 1 - dim))
    return loudness


def gaussian(own_key, dims, deviation, reach, split=(), kind=jnp.bfloat16):
    gain = block_scale(own_key, dims, split, -0.22, 0.18) if split else 1.0
    entries = jax.random.normal(own_key, dims, jnp.float32) * deviation * gain
    return jnp.minimum(jnp.maximum(entries, -reach), reach).astype(kind)


def setup_inputs(seed: int = 0) -> dict:
    splits = jax.random.split(jax.random.key(seed), 10)
    return {
        "tokens": gaussian(splits[0], (SEQS, LEN, D), 1.0, 6.0, ((0, 8), (1, 4))),
        "positions": draw_positions(jax.random.fold_in(splits[9], 71), 0),
        "norm1_gain": jnp.clip(1.0 + 0.1 * jax.random.normal(splits[2], (D,), jnp.float32), 0.5, 1.5).astype(jnp.bfloat16),
        "qkv_weight": draw_qkv_weight(jax.random.fold_in(splits[9], 71), 0),
        "out_weight": gaussian(splits[4], (D, D), (0.036 * LEN ** 0.5), 6.0, ((0, 8),)),
        "norm2_gain": jnp.clip(1.0 + 0.1 * jax.random.normal(splits[5], (D,), jnp.float32), 0.5, 1.5).astype(jnp.bfloat16),
        "in_weight": gaussian(splits[6], (D, 2 * FF), D ** -0.5, 0.21875, ((0, 8),)),
        "down_weight": gaussian(splits[7], (FF, D), FF ** -0.5, 0.1875, ((1, 8),)),
        "cotangent": gaussian(splits[8], (SEQS, LEN, D), 1.0, 6.0, ((0, 8), (1, 4))),
    }


eps = 1e-05
theta = 160000.0

def layer_norm(values, gain_vec):
    middle = lax.optimization_barrier(jnp.mean(values, axis=-1, keepdims=True))
    centred = values - middle
    inverse = lax.rsqrt(lax.optimization_barrier(jnp.mean(centred * centred, axis=-1, keepdims=True)) + eps)
    scaled = centred * inverse
    return (scaled * gain_vec, scaled, inverse)

def norm_back(upstream, scaled, inverse, gain_vec):
    gain_grad = lax.optimization_barrier(jnp.sum(upstream * scaled, axis=0))
    weighted = upstream * gain_vec
    result = inverse * (weighted - lax.optimization_barrier(jnp.mean(weighted, axis=-1, keepdims=True)) - scaled * lax.optimization_barrier(jnp.mean(weighted * scaled, axis=-1, keepdims=True)))
    return (result, gain_grad)

def rotary_tables(positions, head_size):
    half_dim = head_size // 2
    frequency = theta ** (-jnp.arange(half_dim, dtype=jnp.float32) / half_dim)
    angles = positions.astype(jnp.float32)[..., None] * frequency
    return (jnp.cos(angles)[..., None, :], jnp.sin(angles)[..., None, :])

def rotate(values, cosine_table, sine_table):
    half_dim = values.shape[-1] // 2
    first_half = values[..., :half_dim]
    second_half = values[..., half_dim:]
    return jnp.concatenate([first_half * cosine_table - second_half * sine_table, second_half * cosine_table + first_half * sine_table], axis=-1)

def rotate_back(values, cosine_table, sine_table):
    half_dim = values.shape[-1] // 2
    first_half = values[..., :half_dim]
    second_half = values[..., half_dim:]
    return jnp.concatenate([first_half * cosine_table + second_half * sine_table, second_half * cosine_table - first_half * sine_table], axis=-1)

def gelu_slope(values):
    return 0.5 * (1.0 + lax.erf(values * 0.7071067811865476)) + values * jnp.exp(-0.5 * values * values) * 0.3989422804014327

def sequence_pass(weight_set, tokens, positions, cotangent):
    qkv_weight, out_weight, in_weight, down_weight, gain_one, gain_two = weight_set
    score_scale = HEAD_DIM ** (-0.5)
    f32 = jnp.float32
    low = jnp.bfloat16
    inputs = tokens.astype(f32)
    normed_one, scaled_one, inverse_one = layer_norm(inputs, gain_one)
    normed_one = normed_one.astype(low)
    projected = jnp.dot(normed_one, qkv_weight, preferred_element_type=f32).reshape(LEN, 3, HEADS, HEAD_DIM)
    cosine_table, sine_table = rotary_tables(positions, HEAD_DIM)
    queries = rotate(projected[:, 0], cosine_table, sine_table).astype(low)
    key_rows = rotate(projected[:, 1], cosine_table, sine_table).astype(low)
    value_rows = projected[:, 2].astype(low)
    scores = jnp.einsum('qhd,khd->hqk', queries.astype(f32), key_rows.astype(f32)) * score_scale
    totals = jax.nn.logsumexp(scores, axis=-1)
    probs = jnp.exp(scores - totals[..., None])
    probs_low = probs.astype(low)
    attended = jnp.einsum('hqk,khd->qhd', probs_low.astype(f32), value_rows.astype(f32)).astype(low)
    attended_flat = attended.reshape(LEN, D)
    residual = inputs + jnp.dot(attended_flat, out_weight, preferred_element_type=f32)
    normed_two, scaled_two, inverse_two = layer_norm(residual, gain_two)
    normed_two = normed_two.astype(low)
    lifted = jnp.dot(normed_two, in_weight, preferred_element_type=f32)
    act_input = lifted[:, :FF]
    gate_part = lifted[:, FF:]
    activated = jax.nn.gelu(act_input, approximate=False)
    gated = (activated * gate_part).astype(low)
    block_out = (residual + jnp.dot(gated, down_weight, preferred_element_type=f32)).astype(low)
    down_grad = jnp.dot(gated.T, cotangent, preferred_element_type=f32)
    gated_grad = jnp.dot(cotangent, down_weight.T, preferred_element_type=f32)
    lifted_grad = jnp.concatenate([gated_grad * gate_part * gelu_slope(act_input), gated_grad * activated], axis=1).astype(low)
    in_grad = jnp.dot(normed_two.T, lifted_grad, preferred_element_type=f32)
    normed_two_grad = jnp.dot(lifted_grad, in_weight.T, preferred_element_type=f32)
    residual_part, gain_two_grad = norm_back(normed_two_grad, scaled_two, inverse_two, gain_two)
    residual_grad = cotangent.astype(f32) + residual_part
    residual_low = residual_grad.astype(low)
    out_grad = jnp.dot(attended_flat.T, residual_low, preferred_element_type=f32)
    attended_grad = jnp.dot(residual_low, out_weight.T, preferred_element_type=f32).astype(low).reshape(LEN, HEADS, HEAD_DIM)
    grad_f = attended_grad.astype(f32)
    delta_rows = lax.optimization_barrier(jnp.sum(grad_f * attended.astype(f32), axis=-1)).T
    value_grad = jnp.einsum('hqk,qhd->khd', probs_low.astype(f32), grad_f).astype(low)
    prob_grad = jnp.einsum('qhd,khd->hqk', grad_f, value_rows.astype(f32))
    score_grad = (probs * (prob_grad - delta_rows[..., None])).astype(low).astype(f32)
    query_grad = (jnp.einsum('hqk,khd->qhd', score_grad, key_rows.astype(f32)) * score_scale).astype(low)
    key_grad = (jnp.einsum('hqk,qhd->khd', score_grad, queries.astype(f32)) * score_scale).astype(low)
    qkv_grad = jnp.stack([rotate_back(query_grad.astype(f32), cosine_table, sine_table), rotate_back(key_grad.astype(f32), cosine_table, sine_table), value_grad.astype(f32)], axis=1).reshape(LEN, 3 * D).astype(low)
    qkv_grad_w = jnp.dot(normed_one.T, qkv_grad, preferred_element_type=f32)
    normed_one_grad = jnp.dot(qkv_grad, qkv_weight.T, preferred_element_type=f32)
    input_part, gain_one_grad = norm_back(normed_one_grad, scaled_one, inverse_one, gain_one)
    input_grad = (residual_grad + input_part).astype(low)
    return ((block_out, input_grad), (qkv_grad_w, out_grad, in_grad, down_grad, gain_one_grad, gain_two_grad))

def reference(tokens, positions, norm1_gain, qkv_weight, out_weight, norm2_gain, in_weight, down_weight, cotangent):
    weight_set = (qkv_weight, out_weight, in_weight, down_weight, norm1_gain.astype(jnp.float32), norm2_gain.astype(jnp.float32))

    def advance(carry, inputs):
        outputs, grads = sequence_pass(weight_set, inputs[0], inputs[1], inputs[2])
        return (jax.tree.map(lambda left, right: left + right, carry, grads), outputs)
    start = (jnp.zeros((D, 3 * D), jnp.float32), jnp.zeros((D, D), jnp.float32), jnp.zeros((D, 2 * FF), jnp.float32), jnp.zeros((FF, D), jnp.float32), jnp.zeros((D,), jnp.float32), jnp.zeros((D,), jnp.float32))
    grads, outputs = lax.scan(advance, start, (tokens, positions, cotangent))
    return (outputs[0], outputs[1], grads[0], grads[1], grads[2], grads[3], grads[4], grads[5])
```

```python
import functools

import jax
import jax.numpy as jnp
from jax import lax
from jax.experimental import pallas as pl
from jax.experimental.pallas import tpu as pltpu
from jax.sharding import PartitionSpec as P

HEADS = 12
HEAD_DIM = 64
MESH = pl.DeviceIdType.MESH

eps = 1e-05
theta = 160000.0


EXTRA = {"gather": 4, "swap": 3, "spread": 5, "fold": 8, "grad": 11, "reduce": 11}


def exchange_kernel(kinds, seq_n, fsdp_n, *refs):
    f32 = jnp.float32
    count = len(kinds)
    ins = refs[:count]
    outs = refs[count : 2 * count]
    rest = list(refs[2 * count :])
    z = lax.axis_index("seq")
    f = lax.axis_index("fsdp")
    pairs = fsdp_n // 2
    chip = f // 2
    core = f % 2
    partner = chip * 2 + 1 - core
    on_seq = any(kind not in ("spread", "reduce") for kind in kinds)
    on_fsdp = any(kind in ("spread", "grad", "reduce") for kind in kinds)

    barrier = pltpu.get_barrier_semaphore()
    waits = 0
    if on_seq:
        for d in range(1, seq_n):
            pl.semaphore_signal(
                barrier, inc=1, device_id={"seq": (z + d) % seq_n}, device_id_type=MESH
            )
        waits += seq_n - 1
    if on_fsdp:
        for d in range(1, pairs):
            pl.semaphore_signal(
                barrier,
                inc=1,
                device_id={"fsdp": ((chip + d) % pairs) * 2 + core},
                device_id_type=MESH,
            )
        pl.semaphore_signal(barrier, inc=1, device_id={"fsdp": partner}, device_id_type=MESH)
        waits += pairs
    pl.semaphore_wait(barrier, waits)

    def remote(src, dst, send, recv, where):
        return pltpu.make_async_remote_copy(
            src_ref=src,
            dst_ref=dst,
            send_sem=send,
            recv_sem=recv,
            device_id=where,
            device_id_type=MESH,
        )

    groups = {kind: [] for kind in EXTRA}
    for kind, src, dst in zip(kinds, ins, outs):
        groups[kind].append((src, dst, [rest.pop(0) for _ in range(EXTRA[kind])]))
    finish = []
    up = {"seq": lax.rem(z + 1, seq_n)}
    down = {"seq": lax.rem(z + seq_n - 1, seq_n)}
    has_up = z < seq_n - 1
    has_down = z > 0

    def line_start(dst, sems, src):
        up_send, up_recv, down_send, down_recv = sems

        @pl.when(has_up)
        def _():
            remote(src, dst.at[z], up_send.at[0], up_recv.at[1], up).start()

        @pl.when(has_down)
        def _():
            remote(src, dst.at[z], down_send.at[0], down_recv.at[1], down).start()

    def line_step(dst, sems, d):
        up_send, up_recv, down_send, down_recv = sems

        @pl.when(z >= d)
        def _():
            block = dst.at[lax.rem(z + seq_n - d, seq_n)]
            remote(block, block, up_send.at[d], up_recv.at[d], up).wait_recv()
            if d < seq_n - 1:

                @pl.when(has_up)
                def _():
                    remote(block, block, up_send.at[d], up_recv.at[d + 1], up).start()

        @pl.when(z + d < seq_n)
        def _():
            block = dst.at[lax.rem(z + d, seq_n)]
            remote(block, block, down_send.at[d], down_recv.at[d], down).wait_recv()
            if d < seq_n - 1:

                @pl.when(has_down)
                def _():
                    remote(block, block, down_send.at[d], down_recv.at[d + 1], down).start()

    def line_end(dst, sems, src):
        up_send, up_recv, down_send, down_recv = sems
        for d in range(seq_n - 1):

            @pl.when(jnp.logical_and(has_up, z >= d))
            def _():
                block = src if d == 0 else dst.at[lax.rem(z + seq_n - d, seq_n)]
                remote(block, dst.at[z], up_send.at[d], up_recv.at[d + 1], up).wait_send()

            @pl.when(jnp.logical_and(has_down, z + d < seq_n))
            def _():
                block = src if d == 0 else dst.at[lax.rem(z + d, seq_n)]
                remote(block, dst.at[z], down_send.at[d], down_recv.at[d + 1], down).wait_send()

    lower = z * 2 < seq_n

    def fold_steps(k, first):
        t = seq_n - 1 - k
        for src, dst, extra in groups["fold"]:
            up_buf, up_sum, down_buf, down_sum, up_send, up_recv, down_send, down_recv = extra
            near_up = lower if first else jnp.logical_not(lower)

            @pl.when(jnp.logical_and(near_up, jnp.logical_and(z > 0, z < t)))
            def _():
                remote(src.at[t], up_buf.at[t], up_send.at[t], up_recv.at[t], up).wait_recv()
                up_sum[t] = (src[t].astype(f32) + up_buf[t].astype(f32)).astype(src.dtype)
                remote(up_sum.at[t], up_buf.at[t], up_send.at[t], up_recv.at[t], up).start()

            @pl.when(
                jnp.logical_and(
                    jnp.logical_not(near_up), jnp.logical_and(z < seq_n - 1, z > k)
                )
            )
            def _():
                remote(src.at[k], down_buf.at[k], down_send.at[k], down_recv.at[k], down).wait_recv()
                down_sum[k] = (src[k].astype(f32) + down_buf[k].astype(f32)).astype(src.dtype)
                remote(down_sum.at[k], down_buf.at[k], down_send.at[k], down_recv.at[k], down).start()

    for src, dst, extra in groups["grad"] + groups["reduce"]:
        held, total, send_a, recv_a, send_b, recv_b = extra[:6]
        for d in range(pairs):
            block = ((chip + d) % pairs) * 2
            remote(
                src.at[block + 1 - core], held.at[d], send_a.at[d], recv_a.at[d], {"fsdp": partner}
            ).start()
    for src, dst, extra in groups["gather"]:
        line_start(dst, extra, src)
    for k in range(seq_n - 1):
        t = seq_n - 1 - k
        for src, dst, extra in groups["fold"]:
            up_buf, up_sum, down_buf, down_sum, up_send, up_recv, down_send, down_recv = extra

            @pl.when(z == 0)
            def _():
                remote(src.at[t], up_buf.at[t], up_send.at[t], up_recv.at[t], up).start()

            @pl.when(z == seq_n - 1)
            def _():
                remote(src.at[k], down_buf.at[k], down_send.at[k], down_recv.at[k], down).start()

    for src, dst, extra in groups["swap"]:
        send, recv, own = extra
        for d in range(1, seq_n):
            to = (z + d) % seq_n
            piece = src.at[to]
            copy = remote(piece, dst.at[z], send.at[d], recv.at[d], {"seq": to})
            copy.start()
            finish.append(copy.wait_send)
            origin = (z + seq_n - d) % seq_n
            arrival = remote(piece, dst.at[origin], send.at[d], recv.at[d], {"seq": to})
            finish.append(arrival.wait_recv)
        local_copy = pltpu.make_async_copy(src.at[z], dst.at[z], own.at[0])
        local_copy.start()
        finish.append(local_copy.wait)
    for src, dst, extra in groups["spread"]:
        send_a, recv_a, send_b, recv_b, own = extra
        for d in range(1, pairs):
            copy = remote(
                src,
                dst.at[f],
                send_a.at[d],
                recv_a.at[d],
                {"fsdp": ((chip + d) % pairs) * 2 + core},
            )
            copy.start()
            finish.append(copy.wait_send)
        copy = remote(src, dst.at[f], send_b.at[0], recv_b.at[0], {"fsdp": partner})
        copy.start()
        finish.append(copy.wait_send)
        local_copy = pltpu.make_async_copy(src, dst.at[f], own.at[0])
        local_copy.start()
        finish.append(local_copy.wait)
    for src, dst, extra in groups["gather"]:
        dst[z] = src[...]
    for src, dst, extra in groups["grad"] + groups["reduce"]:
        held, total, send_a, recv_a, send_b, recv_b = extra[:6]
        for d in list(range(1, pairs)) + [0]:
            block = ((chip + d) % pairs) * 2
            pair_copy = remote(
                src.at[block + 1 - core], held.at[d], send_a.at[d], recv_a.at[d], {"fsdp": partner}
            )
            pair_copy.wait_recv()
            finish.append(pair_copy.wait_send)
            total[d] = (src[block + core].astype(f32) + held[d].astype(f32)).astype(src.dtype)
            if d > 0:
                copy = remote(
                    total.at[d],
                    extra[10].at[d],
                    send_b.at[d],
                    recv_b.at[d],
                    {"fsdp": block + core},
                )
                copy.start()
                finish.append(copy.wait_send)
    for d in range(1, seq_n):
        for src, dst, extra in groups["gather"]:
            line_step(dst, extra, d)
        for e in range(1, pairs) if d == max(seq_n - 2, 1) else ():
            for src, dst, extra in groups["spread"]:
                send_a, recv_a, send_b, recv_b, own = extra
                origin = ((chip + pairs - e) % pairs) * 2 + core
                remote(src, dst.at[origin], send_a.at[e], recv_a.at[e], {"fsdp": partner}).wait_recv()
                copy = remote(
                    dst.at[origin], dst.at[origin], send_b.at[e], recv_b.at[e], {"fsdp": partner}
                )
                copy.start()
                finish.append(copy.wait_send)
        fold_steps(d - 1, True)
    for k in range(seq_n - 1):
        fold_steps(k, False)

    for j in range(len(groups["grad"]) + seq_n - 1):
        for d in range(1, seq_n):
            if 0 <= j - d < len(groups["grad"]):
                line_step(groups["grad"][j - d][1], groups["grad"][j - d][2][6:10], d)
        if j >= len(groups["grad"]):
            continue
        src, dst, extra = groups["grad"][j]
        held, total, send_a, recv_a, send_b, recv_b = extra[:6]
        value = total[0].astype(f32)
        for d in range(1, pairs):
            remote(
                total.at[d], extra[10].at[d], send_b.at[d], recv_b.at[d], {"fsdp": partner}
            ).wait_recv()
            value = value + extra[10][d].astype(f32)
        dst[z] = value.astype(src.dtype)
        line_start(dst, extra[6:10], dst.at[z])
    for src, dst, extra in groups["reduce"]:
        total, send_b, recv_b = extra[1], extra[4], extra[5]
        value = total[0].astype(f32)
        for d in range(1, pairs):
            remote(
                total.at[d], extra[10].at[d], send_b.at[d], recv_b.at[d], {"fsdp": partner}
            ).wait_recv()
            value = value + extra[10][d].astype(f32)
        dst[...] = value.astype(src.dtype)
    for src, dst, extra in groups["fold"]:
        up_buf, up_sum, down_buf, down_sum, up_send, up_recv, down_send, down_recv = extra
        dst[...] = src[z].astype(f32)

        @pl.when(z > 0)
        def _():
            remote(src.at[z], up_buf.at[z], up_send.at[z], up_recv.at[z], up).wait_recv()
            dst[...] += up_buf[z].astype(f32)

        @pl.when(z < seq_n - 1)
        def _():
            remote(src.at[z], down_buf.at[z], down_send.at[z], down_recv.at[z], down).wait_recv()
            dst[...] += down_buf[z].astype(f32)

        for t in range(seq_n):

            @pl.when(z < t)
            def _():
                remote(src.at[t], up_buf.at[t], up_send.at[t], up_recv.at[t], up).wait_send()

            @pl.when(z > t)
            def _():
                remote(src.at[t], down_buf.at[t], down_send.at[t], down_recv.at[t], down).wait_send()

    for src, dst, extra in groups["spread"]:
        send_a, recv_a, send_b, recv_b, own = extra
        for d in range(pairs):
            origin = ((chip + pairs - d) % pairs) * 2 + 1 - core
            finish.append(
                remote(src, dst.at[origin], send_b.at[d], recv_b.at[d], {"fsdp": partner}).wait_recv
            )
    for wait in finish:
        wait()
    for src, dst, extra in groups["gather"]:
        line_end(dst, extra, src)
    for src, dst, extra in groups["grad"]:
        line_end(dst, extra[6:10], dst.at[z])


def exchange(kinds, arrays, collective_id):
    seq_n = lax.axis_size("seq")
    fsdp_n = lax.axis_size("fsdp")
    pairs = fsdp_n // 2
    results = []
    scratch = []
    dma = pltpu.SemaphoreType.DMA
    for kind, array in zip(kinds, arrays):
        dtype = array.dtype
        if kind == "gather":
            shape = (seq_n,) + array.shape
            scratch += [dma((seq_n,))] * 4
        elif kind == "swap":
            shape = array.shape
            scratch += [dma((seq_n,)), dma((seq_n,)), dma((1,))]
        elif kind == "fold":
            shape = array.shape[1:]
            scratch += [pltpu.VMEM(array.shape, dtype)] * 4 + [dma((seq_n,))] * 4
            dtype = jnp.float32
        elif kind == "spread":
            shape = (fsdp_n,) + array.shape
            scratch += [dma((pairs,))] * 4 + [dma((1,))]
        else:
            shape = array.shape[1:]
            if kind == "grad":
                shape = (seq_n,) + shape
            half = pltpu.VMEM((pairs,) + array.shape[1:], dtype)
            scratch += [half] * 2 + [dma((pairs,))] * 4 + [dma((seq_n,))] * 4 + [half]
        results.append(jax.ShapeDtypeStruct(shape, dtype))
    space = pl.BlockSpec(memory_space=pltpu.VMEM)
    return pl.pallas_call(
        functools.partial(exchange_kernel, tuple(kinds), seq_n, fsdp_n),
        out_shape=results,
        in_specs=[space] * len(kinds),
        out_specs=[space] * len(kinds),
        scratch_shapes=scratch,
        compiler_params=pltpu.CompilerParams(collective_id=collective_id, has_side_effects=True),
        name=f"exchange_{collective_id}",
    )(*arrays)


def layer_norm(values, gain_vec):
    middle = jnp.mean(values, axis=-1, keepdims=True)
    centred = values - middle
    inverse = lax.rsqrt(jnp.mean(centred * centred, axis=-1, keepdims=True) + eps)
    scaled = centred * inverse
    return (scaled * gain_vec, scaled, inverse)


def norm_back(upstream, scaled, inverse, gain_vec):
    weighted = upstream * gain_vec
    return inverse * (
        weighted
        - jnp.mean(weighted, axis=-1, keepdims=True)
        - scaled * jnp.mean(weighted * scaled, axis=-1, keepdims=True)
    )


def rotary_tables(positions, head_size):
    half_dim = head_size // 2
    frequency = theta ** (-jnp.arange(half_dim, dtype=jnp.float32) / half_dim)
    angles = positions.astype(jnp.float32)[..., None] * frequency
    return (jnp.cos(angles), jnp.sin(angles))


def rotate(values, cosine_table, sine_table):
    half_dim = values.shape[-1] // 2
    first_half = values[..., :half_dim]
    second_half = values[..., half_dim:]
    return jnp.concatenate(
        [
            first_half * cosine_table - second_half * sine_table,
            second_half * cosine_table + first_half * sine_table,
        ],
        axis=-1,
    )


def gelu_slope(values):
    return (
        0.5 * (1.0 + lax.erf(values * 0.7071067811865476))
        + values * jnp.exp(-0.5 * values * values) * 0.3989422804014327
    )


def dot(left, right, left_dim=1, right_dim=0):
    return lax.dot_general(
        left, right, (((left_dim,), (right_dim,)), ((), ())), preferred_element_type=jnp.float32
    )


def local(
    tokens,
    positions,
    norm1_gain,
    qkv_weight,
    out_weight,
    norm2_gain,
    in_weight,
    down_weight,
    cotangent,
):
    f32 = jnp.float32
    low = jnp.bfloat16
    groups = lax.axis_size("seq")
    fsdp_n = lax.axis_size("fsdp")
    z = lax.axis_index("seq")
    seq_dev, span_len, width = tokens.shape
    rows = seq_dev * span_len
    length = span_len * groups
    local_heads = HEADS // groups
    group_width = local_heads * HEAD_DIM
    shard = qkv_weight.shape[0]
    ff = down_weight.shape[0]
    ff_part = ff // groups
    scale = HEAD_DIM ** (-0.5)

    def pick(weight, sections, section):
        part = None
        for g in range(groups):
            columns = [
                weight[:, (j * groups + g) * section : (j * groups + g + 1) * section]
                for j in range(sections)
            ]
            own = jnp.concatenate(columns, axis=1)
            part = own if part is None else jnp.where(z == g, own, part)
        return part

    qkv_part = pick(qkv_weight, 3, group_width)
    in_part = pick(in_weight, 2, ff_part)
    down_part = lax.dynamic_slice_in_dim(down_weight, z * ff_part, ff_part, 0).T
    gains = jnp.stack([norm1_gain, norm2_gain])
    own_tokens = tokens.reshape(rows, width)
    own_cotangent = cotangent.reshape(rows, width)

    def whole(stack):
        w = stack.shape[-1]
        return jnp.swapaxes(stack.reshape(groups, seq_dev, span_len, w), 0, 1).reshape(
            seq_dev * length, w
        )

    def spans(full):
        w = full.shape[-1]
        return jnp.swapaxes(full.reshape(seq_dev, groups, span_len, w), 0, 1).reshape(
            groups, rows, w
        )

    all_tokens, all_cot, all_pos, w_qkv, w_out, w_in, w_down, all_gains = exchange(
        ["gather", "gather", "gather", "spread", "spread", "spread", "spread", "spread"],
        [own_tokens, own_cotangent, positions, qkv_part, out_weight, in_part, down_part, gains],
        0,
    )
    all_tokens = whole(all_tokens)
    all_cot = whole(all_cot)
    all_pos = jnp.swapaxes(all_pos, 0, 1).reshape(seq_dev, length)
    w_qkv = w_qkv.reshape(width, 3 * group_width)
    w_out = w_out.reshape(width, width)
    w_in = w_in.reshape(width, 2 * ff_part)
    w_down = w_down.reshape(width, ff_part)
    gain_one = all_gains[:, 0].reshape(width).astype(f32)
    gain_two = all_gains[:, 1].reshape(width).astype(f32)

    normed_one, scaled_full, _ = layer_norm(all_tokens.astype(f32), gain_one)
    normed_one = normed_one.astype(low)
    projected = dot(normed_one, w_qkv).reshape(seq_dev, length, 3, local_heads, HEAD_DIM)
    projected = projected.transpose(2, 0, 3, 1, 4)
    cosine, sine = rotary_tables(all_pos, HEAD_DIM)
    cosine = cosine[:, None]
    sine = sine[:, None]
    query = rotate(projected[0], cosine, sine).astype(low)
    key = rotate(projected[1], cosine, sine).astype(low)
    value = projected[2].astype(low)
    scores = jnp.einsum("bhqd,bhkd->bhqk", query, key, preferred_element_type=f32) * scale
    totals = jax.nn.logsumexp(scores, axis=-1, keepdims=True)
    probs = jnp.exp(scores - totals)
    probs_low = probs.astype(low)
    attended = jnp.einsum("bhqk,bhkd->bhqd", probs_low, value, preferred_element_type=f32).astype(
        low
    )

    def to_rows(heads):
        return jnp.concatenate([heads[:, h] for h in range(local_heads)], axis=-1).reshape(
            seq_dev * length, group_width
        )

    (mixed,) = exchange(["swap"], [spans(to_rows(attended))], 1)
    w_out = w_out.reshape(groups, group_width, width)
    inputs = own_tokens.astype(f32)
    residual = inputs + jnp.einsum("grd,gdw->rw", mixed, w_out, preferred_element_type=f32)
    normed_two, scaled_two, inverse_two = layer_norm(residual, gain_two)
    normed_two = normed_two.astype(low)
    (normed_full,) = exchange(["gather"], [normed_two], 2)
    normed_full = whole(normed_full)
    lifted = dot(normed_full, w_in)
    act = lifted[:, :ff_part]
    gate = lifted[:, ff_part:]
    activated = jax.nn.gelu(act, approximate=False)
    gated = (activated * gate).astype(low)
    gated_grad = dot(all_cot, w_down)
    lifted_grad = jnp.concatenate(
        [gated_grad * gate * gelu_slope(act), gated_grad * activated], axis=1
    ).astype(low)
    ffn_part = dot(gated, w_down, 1, 1).astype(low)
    normed_grad_part = dot(lifted_grad, w_in, 1, 1).astype(low)
    in_term = dot(normed_full, lifted_grad, 0, 0).astype(low)
    down_term = dot(all_cot, gated, 0, 0).astype(low)

    def by_owner(term):
        return term.reshape(fsdp_n, shard, term.shape[1])

    normed_two_grad, in_owned, down_owned = exchange(
        ["fold", "reduce", "reduce"],
        [spans(normed_grad_part), by_owner(in_term), by_owner(down_term)],
        3,
    )
    gain_two_grad = jnp.sum(normed_two_grad * scaled_two, axis=0)
    residual_grad = own_cotangent.astype(f32) + norm_back(
        normed_two_grad, scaled_two, inverse_two, gain_two
    )
    residual_low = residual_grad.astype(low)
    mixed_grad = jnp.einsum("rw,gdw->grd", residual_low, w_out, preferred_element_type=f32)
    out_term = jnp.einsum("grd,rw->gdw", mixed, residual_low, preferred_element_type=f32)
    out_term = out_term.astype(low).reshape(width, width)
    head_grad, out_owned = exchange(
        ["swap", "reduce"], [mixed_grad.astype(low), by_owner(out_term)], 4
    )
    head_grad = whole(head_grad).reshape(seq_dev, length, local_heads, HEAD_DIM)
    head_grad = head_grad.transpose(0, 2, 1, 3)
    delta = jnp.sum(head_grad.astype(f32) * attended.astype(f32), axis=-1, keepdims=True)
    value_grad = jnp.einsum("bhqk,bhqd->bhkd", probs_low, head_grad, preferred_element_type=f32)
    prob_grad = jnp.einsum("bhqd,bhkd->bhqk", head_grad, value, preferred_element_type=f32)
    score_grad = (probs * (prob_grad - delta)).astype(low)
    query_grad = jnp.einsum("bhqk,bhkd->bhqd", score_grad, key, preferred_element_type=f32) * scale
    key_grad = jnp.einsum("bhqk,bhqd->bhkd", score_grad, query, preferred_element_type=f32) * scale
    qkv_grad = jnp.concatenate(
        [
            to_rows(rotate(query_grad.astype(low).astype(f32), cosine, -sine).astype(low)),
            to_rows(rotate(key_grad.astype(low).astype(f32), cosine, -sine).astype(low)),
            to_rows(value_grad.astype(low)),
        ],
        axis=1,
    )
    normed_one_grad_part = dot(qkv_grad, w_qkv, 1, 1)
    gain_one_grad = jnp.sum(normed_one_grad_part * scaled_full, axis=0)

    qkv_term = dot(normed_one, qkv_grad, 0, 0).astype(low)
    gain_terms = jnp.stack(
        [gain_one_grad.reshape(fsdp_n, shard), gain_two_grad.reshape(fsdp_n, shard)], axis=1
    )
    parts = exchange(
        ["fold", "fold", "gather", "gather", "gather", "grad", "grad"],
        [spans(normed_one_grad_part.astype(low)), spans(ffn_part)]
        + [in_owned, down_owned, out_owned, by_owner(qkv_term), gain_terms],
        5,
    )
    normed_one_grad = parts[0]
    _, scaled_one, inverse_one = layer_norm(inputs, gain_one)
    input_grad = (
        residual_grad + norm_back(normed_one_grad, scaled_one, inverse_one, gain_one)
    ).astype(low)
    block_out = (residual + parts[1]).astype(low)
    in_all, down_all, out_all, qkv_all, gain_all = parts[2:]

    def columns_of(stack, sections, section):
        return jnp.concatenate(
            [
                stack[g][:, j * section : (j + 1) * section]
                for j in range(sections)
                for g in range(groups)
            ],
            axis=1,
        ).astype(f32)

    qkv_out = columns_of(qkv_all, 3, group_width)
    in_out = columns_of(in_all, 2, ff_part)
    down_out = down_all.transpose(0, 2, 1).reshape(ff, shard).astype(f32)
    out_out = jnp.sum(out_all.astype(f32), axis=0)
    gain_out = jnp.sum(gain_all, axis=0)
    return (
        block_out.reshape(seq_dev, span_len, width),
        input_grad.reshape(seq_dev, span_len, width),
        qkv_out,
        out_out,
        in_out,
        down_out,
        gain_out[0],
        gain_out[1],
    )


def fused_kernel(dims, *refs):
    seq_n, fsdp_n, heads, chunk = dims
    f32 = jnp.float32
    low = jnp.bfloat16
    names = (
        "tokens", "pos", "gains", "freq", "qkv", "out", "inw", "down", "cot", "block_out",
        "input_grad", "qkv_grad", "out_grad", "in_grad", "down_grad", "gain_grad", "tok_all",
        "pos_all", "gains_all", "qkv_src", "w_qkv", "w_out", "w_in", "w_dn", "xhat", "n1",
        "n1t", "cosine", "sine", "q_m", "k_s", "k_m", "v_s", "v_m", "p_s", "att", "mixed",
        "mgrad", "hgrad", "hg_m", "gain_s", "rg_s", "res_s", "n2t", "cott", "gated",
        "lifted_grad", "dq", "dk", "dv", "g_s", "nog", "up_buf", "up_sum", "down_buf",
        "down_sum", "qkv_own", "qkv_all", "fsum", "gpart", "gq", "gz", "gzall", "t_qkv",
        "h_qkv", "r_qkv", "t_out", "h_out", "r_out", "t_in", "h_in", "r_in", "t_dn", "h_dn",
        "r_dn", "a_out", "a_in", "a_dn", "sem_tok", "sem_pos", "sem_gain", "sem_wq", "sem_wo",
        "sem_wi", "sem_wd", "sem_sw1", "sem_sw2", "sem_fold", "sem_qa", "sem_g", "sem_rq",
        "sem_ro", "sem_ri", "sem_rd", "sem_ao", "sem_ai", "sem_ad",
    )
    assert len(names) == len(refs)
    R = dict(zip(names, refs))
    z = lax.axis_index("seq")
    f = lax.axis_index("fsdp")
    chip = f // 2
    core = f % 2
    px = chip % 2
    py = chip // 2
    flip = [chip, py * 2 + 1 - px, (1 - py) * 2 + px, (1 - py) * 2 + 1 - px]
    partner = {"fsdp": chip * 2 + 1 - core}
    span, width = R["tokens"].shape
    shard = R["out"].shape[0]
    group_width = R["att"].shape[2]
    head_dim = group_width // heads
    half_dim = head_dim // 2
    ff = R["down"].shape[1]
    scale = head_dim ** (-0.5)
    half = shard // 2

    barrier = pltpu.get_barrier_semaphore()
    for d in range(1, seq_n):
        pl.semaphore_signal(
            barrier, inc=1, device_id={"seq": (z + d) % seq_n}, device_id_type=MESH
        )
    for d in range(1, fsdp_n):
        pl.semaphore_signal(
            barrier, inc=1, device_id={"fsdp": (f + d) % fsdp_n}, device_id_type=MESH
        )
    pl.semaphore_wait(barrier, seq_n + fsdp_n - 2)

    finish = []

    def remote(src, dst, send, recv, where):
        return pltpu.make_async_remote_copy(
            src_ref=src,
            dst_ref=dst,
            send_sem=send,
            recv_sem=recv,
            device_id=where,
            device_id_type=MESH,
        )

    def send(src, dst, send_sem, recv_sem, where):
        copy = remote(src, dst, send_sem, recv_sem, where)
        copy.start()
        finish.append(copy.wait_send)

    def await_recv(dst, send_sem, recv_sem, where):
        remote(dst, dst, send_sem, recv_sem, where).wait_recv()

    up = {"seq": lax.rem(z + 1, seq_n)}
    down = {"seq": lax.rem(z + seq_n - 1, seq_n)}
    has_up = z < seq_n - 1
    has_down = z > 0

    def small_start(axis, count, me, src, dst, sems):
        dst[me] = src[...]
        for d in range(1, count):
            send(src, dst.at[me], sems.at[0, d], sems.at[1, d], {axis: (me + d) % count})

    def small_wait(axis, count, me, dst, sems):
        for d in range(1, count):
            origin = (me + count - d) % count
            await_recv(dst.at[origin], sems.at[0, d], sems.at[1, d], {axis: origin})

    def line_start(dst, sems, src):
        dst[z] = src[...]

        @pl.when(has_up)
        def _():
            remote(src, dst.at[z], sems.at[0, 0], sems.at[1, 1], up).start()

        @pl.when(has_down)
        def _():
            remote(src, dst.at[z], sems.at[2, 0], sems.at[3, 1], down).start()

    def line_step(dst, sems, d):
        @pl.when(z >= d)
        def _():
            block = dst.at[lax.rem(z + seq_n - d, seq_n)]
            remote(block, block, sems.at[0, d], sems.at[1, d], up).wait_recv()
            if d < seq_n - 1:

                @pl.when(has_up)
                def _():
                    remote(block, block, sems.at[0, d], sems.at[1, d + 1], up).start()

        @pl.when(z + d < seq_n)
        def _():
            block = dst.at[lax.rem(z + d, seq_n)]
            remote(block, block, sems.at[2, d], sems.at[3, d], down).wait_recv()
            if d < seq_n - 1:

                @pl.when(has_down)
                def _():
                    remote(block, block, sems.at[2, d], sems.at[3, d + 1], down).start()

    def line_end(dst, sems, src):
        for d in range(seq_n - 1):

            @pl.when(jnp.logical_and(has_up, z >= d))
            def _():
                block = src if d == 0 else dst.at[lax.rem(z + seq_n - d, seq_n)]
                remote(block, dst.at[z], sems.at[0, d], sems.at[1, d + 1], up).wait_send()

            @pl.when(jnp.logical_and(has_down, z + d < seq_n))
            def _():
                block = src if d == 0 else dst.at[lax.rem(z + d, seq_n)]
                remote(block, dst.at[z], sems.at[2, d], sems.at[3, d + 1], down).wait_send()

    def spread_start(src, dst, sems):
        for nb in (1, 2):
            send(src, dst.at[f], sems.at[0, nb], sems.at[1, nb], {"fsdp": flip[nb] * 2 + core})
        send(src, dst.at[f], sems.at[2, 0], sems.at[3, 0], partner)
        dst[f] = src[...]

    def spread_one(dst, sems):
        for nb in (1, 2):
            origin = flip[nb] * 2 + core
            await_recv(dst.at[origin], sems.at[0, nb], sems.at[1, nb], partner)
            part = dst.at[origin, pl.ds((nb - 1) * half, half)]
            send(part, part, sems.at[4, nb], sems.at[5, nb], {"fsdp": flip[3 - nb] * 2 + core})
            send(dst.at[origin], dst.at[origin], sems.at[2, nb], sems.at[3, nb], partner)

    def spread_two(dst, sems):
        origin = flip[3] * 2 + core
        for nb in (1, 2):
            part = dst.at[origin, pl.ds((nb - 1) * half, half)]
            await_recv(part, sems.at[4, nb], sems.at[5, nb], partner)
        send(dst.at[origin], dst.at[origin], sems.at[2, 3], sems.at[3, 3], partner)

    def spread_wait(dst, sems):
        for e in range(4):
            origin = flip[e] * 2 + 1 - core
            await_recv(dst.at[origin], sems.at[2, e], sems.at[3, e], partner)

    def swap_start(src, dst, sems):
        for d in range(1, seq_n):
            to = (z + d) % seq_n
            send(src.at[to], dst.at[z], sems.at[0, d], sems.at[1, d], {"seq": to})
        dst[z] = src[z]

    def swap_wait(dst, sems):
        for d in range(1, seq_n):
            origin = (z + seq_n - d) % seq_n
            await_recv(dst.at[origin], sems.at[0, d], sems.at[1, d], {"seq": origin})

    def pair_start(key, sems):
        src, held = R["t_" + key], R["h_" + key]
        for d in (3, 1, 2, 0):
            send(src.at[flip[d] * 2 + 1 - core], held.at[d], sems.at[0, d], sems.at[1, d], partner)

    def pair_add(key, sems):
        src, held = R["t_" + key], R["h_" + key]
        for d in (3, 1, 2, 0):
            await_recv(held.at[d], sems.at[0, d], sems.at[1, d], partner)
            held[d] = (src[flip[d] * 2 + core].astype(f32) + held[d].astype(f32)).astype(low)
            if d > 0:
                send(
                    held.at[d],
                    R["r_" + key].at[d],
                    sems.at[2, d],
                    sems.at[3, d],
                    {"fsdp": flip[d] * 2 + core},
                )

    def plane_sum(key, sems):
        total, got = R["h_" + key], R["r_" + key]
        for d in (1, 2, 3):
            await_recv(got.at[d], sems.at[2, d], sems.at[3, d], partner)
        return (
            total[0].astype(f32) + got[1].astype(f32) + got[2].astype(f32) + got[3].astype(f32)
        ).astype(low)

    mid = seq_n // 2
    lower = z < mid
    depth = jnp.where(lower, z, seq_n - 1 - z)
    inner = {"seq": jnp.where(lower, z + 1, z - 1)}
    outer = {"seq": jnp.where(lower, lax.rem(z + seq_n - 1, seq_n), lax.rem(z + 1, seq_n))}

    def all_first(key, sems, psems):
        buf = R["a_" + key]
        buf[0] = plane_sum(key, psems)

        @pl.when(depth == 0)
        def _():
            remote(buf.at[0], buf.at[1], sems.at[0, 0], sems.at[1, 0], inner).start()

    def all_mid(key, sems):
        buf = R["a_" + key]

        @pl.when(depth > 0)
        def _():
            remote(buf.at[1], buf.at[1], sems.at[0, 0], sems.at[1, 0], outer).wait_recv()
            buf[2] = (buf[0].astype(f32) + buf[1].astype(f32)).astype(low)

            @pl.when(depth < mid - 1)
            def _():
                remote(buf.at[2], buf.at[1], sems.at[0, 0], sems.at[1, 0], inner).start()

            @pl.when(depth == mid - 1)
            def _():
                remote(buf.at[2], buf.at[3], sems.at[0, 1], sems.at[1, 1], inner).start()

    def all_cross(key, sems):
        buf = R["a_" + key]

        @pl.when(depth == mid - 1)
        def _():
            remote(buf.at[3], buf.at[3], sems.at[0, 1], sems.at[1, 1], inner).wait_recv()
            buf[4] = (buf[2].astype(f32) + buf[3].astype(f32)).astype(low)
            remote(buf.at[4], buf.at[4], sems.at[0, 2], sems.at[1, 2], outer).start()

    def all_last(key, sems):
        buf = R["a_" + key]

        @pl.when(depth < mid - 1)
        def _():
            remote(buf.at[4], buf.at[4], sems.at[0, 2], sems.at[1, 2], inner).wait_recv()

            @pl.when(depth > 0)
            def _():
                remote(buf.at[4], buf.at[4], sems.at[0, 2], sems.at[1, 2], outer).start()

    def all_end(key, sems):
        buf = R["a_" + key]

        @pl.when(depth == 0)
        def _():
            remote(buf.at[0], buf.at[1], sems.at[0, 0], sems.at[1, 0], inner).wait_send()

        @pl.when(depth > 0)
        def _():
            @pl.when(depth < mid - 1)
            def _():
                remote(buf.at[2], buf.at[1], sems.at[0, 0], sems.at[1, 0], inner).wait_send()

            @pl.when(depth == mid - 1)
            def _():
                remote(buf.at[2], buf.at[3], sems.at[0, 1], sems.at[1, 1], inner).wait_send()

            remote(buf.at[4], buf.at[4], sems.at[0, 2], sems.at[1, 2], outer).wait_send()

    small_start("seq", seq_n, z, R["pos"], R["pos_all"], R["sem_pos"])
    small_start("fsdp", fsdp_n, f, R["gains"], R["gains_all"], R["sem_gain"])
    line_start(R["tok_all"], R["sem_tok"], R["tokens"])
    for g in range(seq_n):

        @pl.when(z == g)
        def _():
            for j in range(3):
                at = (j * seq_n + g) * group_width
                R["qkv_src"][:, j * group_width : (j + 1) * group_width] = R["qkv"][
                    :, at : at + group_width
                ]

    spread_start(R["qkv_src"], R["w_qkv"], R["sem_wq"])
    spread_start(R["out"], R["w_out"], R["sem_wo"])

    lane = lax.broadcasted_iota(jnp.int32, (1, 128), 1)
    first = lax.rem(lane, head_dim) < half_dim

    def turn(values, rows, sign):
        pieces = []
        for c in range(values.shape[1] // 128):
            u = values[:, c * 128 : (c + 1) * 128]
            w = jnp.where(
                first, pltpu.roll(u, 128 - half_dim, 1), pltpu.roll(u, half_dim, 1)
            )
            pieces.append(u * R["cosine"][rows] + sign * (w * R["sine"][rows]))
        return jnp.concatenate(pieces, axis=1)

    wide = lax.broadcasted_iota(jnp.int32, (1, 256), 1)

    def masked(values, h):
        at = lax.broadcasted_iota(jnp.int32, values.shape, 1)
        keep = jnp.logical_and(at >= h * head_dim, at < (h + 1) * head_dim)
        return jnp.where(keep, values, 0.0).astype(low)

    def norm(values):
        centred = values - jnp.mean(values, axis=-1, keepdims=True)
        inverse = lax.rsqrt(jnp.mean(centred * centred, axis=-1, keepdims=True) + eps)
        return centred * inverse, inverse

    def norm_block(b):
        scaled, _ = norm(R["tok_all"][b].astype(f32))
        R["xhat"][b] = scaled
        normed = (scaled * R["gain_s"][0:1]).astype(low)
        R["n1"][b] = normed
        R["n1t"][b] = normed.astype(f32).T.astype(low).reshape(fsdp_n, shard, span)

    def project_block(b):
        got = dot(R["n1"][b], R["w_qkv"][...].reshape(width, 3 * group_width))
        row = R["pos_all"][b].astype(f32)
        angle = jnp.broadcast_to(row, (128, span)).T * R["freq"][...]
        R["cosine"][b] = jnp.cos(angle)
        sine = jnp.sin(angle)
        R["sine"][b] = jnp.where(first, -sine, sine)
        q = turn(got[:, 0:256], b, 1.0).astype(low).astype(f32)
        k = turn(pltpu.roll(got[:, 128:512], 384 - 64, 1)[:, 0:256], b, 1.0).astype(low)
        k = jnp.where(wide < group_width, k.astype(f32), 0.0)
        v = got[:, 2 * group_width :].astype(low).astype(f32)
        R["k_s"][b] = k.astype(low)
        R["v_s"][b] = v.astype(low)
        for h in range(heads):
            R["q_m"][h, b] = masked(q, h)
            R["k_m"][h, b] = masked(k, h)
            R["v_m"][h, b] = masked(v, h)

    spread_one(R["w_qkv"], R["sem_wq"])
    spread_start(R["inw"], R["w_in"], R["sem_wi"])
    small_wait("seq", seq_n, z, R["pos_all"], R["sem_pos"])
    small_wait("fsdp", fsdp_n, f, R["gains_all"], R["sem_gain"])
    gains = R["gains_all"][0].astype(f32)
    for e in range(1, fsdp_n):
        gains = gains + R["gains_all"][e].astype(f32)
    R["gain_s"][...] = gains
    norm_block(z)
    line_step(R["tok_all"], R["sem_tok"], 1)
    spread_one(R["w_out"], R["sem_wo"])
    spread_start(R["down"], R["w_dn"], R["sem_wd"])
    spread_two(R["w_qkv"], R["sem_wq"])
    spread_wait(R["w_qkv"], R["sem_wq"])
    project_block(z)
    for d in range(1, seq_n):
        if d > 1:
            line_step(R["tok_all"], R["sem_tok"], d)

        def arrived(side, carry):
            block = jnp.where(side == 0, z - d, z + d)

            @pl.when(jnp.logical_and(block >= 0, block < seq_n))
            def _():
                b = lax.rem(block + seq_n, seq_n)
                norm_block(b)
                project_block(b)

            return carry

        lax.fori_loop(0, 2, arrived, 0)

    length = span * seq_n

    def forward_rows(b, carry):
        result = None
        for h in range(heads):
            scores = dot(R["q_m"][h, b], R["k_s"][...].reshape(length, 256), 1, 1) * scale
            top = jnp.max(scores, axis=-1, keepdims=True)
            exps = jnp.exp(scores - top)
            probs = exps / jnp.sum(exps, axis=-1, keepdims=True)
            R["p_s"][h, b] = probs
            piece = dot(probs.astype(low), R["v_m"][h].reshape(length, group_width))
            result = piece if result is None else result + piece
        R["att"][b] = result.astype(low)
        return carry

    lax.fori_loop(0, seq_n, forward_rows, 0)
    swap_start(R["att"], R["mixed"], R["sem_sw1"])
    spread_one(R["w_in"], R["sem_wi"])
    spread_two(R["w_out"], R["sem_wo"])
    spread_wait(R["w_out"], R["sem_wo"])
    cot = R["cot"][...]
    R["cott"][...] = cot.astype(f32).T.astype(low).reshape(fsdp_n, shard, span)
    spread_one(R["w_dn"], R["sem_wd"])

    swap_wait(R["mixed"], R["sem_sw1"])
    w_out = R["w_out"][...].reshape(width, width)
    residual = R["tokens"][...].astype(f32)
    for g in range(seq_n):
        residual = residual + dot(
            R["mixed"][g], w_out[g * group_width : (g + 1) * group_width]
        )
    R["res_s"][...] = residual
    scaled_two, inverse_two = norm(residual)
    normed_two = (scaled_two * R["gain_s"][1:2]).astype(low)
    R["n2t"][...] = normed_two.astype(f32).T.astype(low).reshape(fsdp_n, shard, span)
    spread_two(R["w_in"], R["sem_wi"])
    spread_wait(R["w_in"], R["sem_wi"])
    spread_two(R["w_dn"], R["sem_wd"])
    spread_wait(R["w_dn"], R["sem_wd"])

    for c in range(0, ff, chunk):
        a = dot(normed_two, R["w_in"][:, :, c : c + chunk].reshape(width, chunk))
        g = dot(normed_two, R["w_in"][:, :, ff + c : ff + c + chunk].reshape(width, chunk))
        gg = dot(cot, R["w_dn"][:, :, c : c + chunk].reshape(width, chunk))
        cdf = 0.5 * (1.0 + lax.erf(a * 0.7071067811865476))
        activated = a * cdf
        slope = cdf + a * jnp.exp(-0.5 * a * a) * 0.3989422804014327
        R["gated"][:, c : c + chunk] = (activated * g).astype(low)
        R["lifted_grad"][:, c : c + chunk] = (gg * g * slope).astype(low)
        R["lifted_grad"][:, ff + c : ff + c + chunk] = (gg * activated).astype(low)
    lifted_grad = R["lifted_grad"][...]
    gated = R["gated"][...]
    normed_two_grad = dot(lifted_grad, R["w_in"][...].reshape(width, 2 * ff), 1, 1)
    R["gpart"][1:2] = jnp.sum(normed_two_grad * scaled_two, axis=0, keepdims=True)

    def norm_back_rows(upstream, scaled, inverse, gain_vec):
        weighted = upstream * gain_vec
        return inverse * (
            weighted
            - jnp.mean(weighted, axis=-1, keepdims=True)
            - scaled * jnp.mean(weighted * scaled, axis=-1, keepdims=True)
        )

    residual_grad = cot.astype(f32) + norm_back_rows(
        normed_two_grad, scaled_two, inverse_two, R["gain_s"][1:2]
    )
    R["rg_s"][...] = residual_grad
    residual_low = residual_grad.astype(low)
    for g in range(seq_n):
        R["mgrad"][g] = dot(
            residual_low, w_out[g * group_width : (g + 1) * group_width], 1, 1
        ).astype(low)
    swap_start(R["mgrad"], R["hgrad"], R["sem_sw2"])

    def down_rows(e, carry):
        R["t_dn"][e] = dot(R["cott"][e], R["gated"][...]).astype(low)
        return carry

    lax.fori_loop(0, fsdp_n, down_rows, 0)
    pair_start("dn", R["sem_rd"])

    def in_rows(e, carry):
        R["t_in"][e] = dot(R["n2t"][e], R["lifted_grad"][...]).astype(low)
        return carry

    lax.fori_loop(0, fsdp_n, in_rows, 0)
    pair_start("in", R["sem_ri"])
    own = group_width // shard
    for g in range(seq_n):
        R["t_out"][g * own : (g + 1) * own] = (
            dot(R["mixed"][g], residual_low, 0, 0).astype(low).reshape(own, shard, width)
        )
    pair_start("out", R["sem_ro"])
    pair_add("dn", R["sem_rd"])

    swap_wait(R["hgrad"], R["sem_sw2"])
    for h in range(heads):
        for b in range(seq_n):
            R["hg_m"][h, b] = masked(R["hgrad"][b].astype(f32), h)
    R["dk"][...] = jnp.zeros(R["dk"].shape, f32)
    R["dv"][...] = jnp.zeros(R["dv"].shape, f32)

    def backward_rows(b, carry):
        grad_q = None
        attended = R["att"][b].astype(f32)
        for h in range(heads):
            probs = R["p_s"][h, b]
            upstream = R["hg_m"][h, b]
            delta = jnp.sum(upstream.astype(f32) * attended, axis=-1, keepdims=True)
            prob_grad = dot(upstream, R["v_s"][...].reshape(length, group_width), 1, 1)
            score_grad = (probs * (prob_grad - delta)).astype(low)
            piece = dot(score_grad, R["k_m"][h].reshape(length, 256))
            grad_q = piece if grad_q is None else grad_q + piece
            R["dk"][...] += dot(score_grad, R["q_m"][h, b], 0, 0)
            R["dv"][...] += dot(probs.astype(low), upstream, 0, 0)
        R["dq"][b] = grad_q
        return carry

    lax.fori_loop(0, seq_n // 2, backward_rows, 0)
    pair_add("in", R["sem_ri"])
    lax.fori_loop(seq_n // 2, seq_n, backward_rows, 0)
    pair_add("out", R["sem_ro"])

    def settle(b, carry):
        rows = pl.ds(pl.multiple_of(b * span, span), span)
        grad_q = turn((R["dq"][b] * scale).astype(low).astype(f32), b, -1.0)
        grad_k = turn((R["dk"][rows] * scale).astype(low).astype(f32), b, -1.0)
        shifted = pltpu.roll(grad_k, 64, 1)
        g = R["g_s"]
        g[b, :, 0:128] = grad_q[:, 0:128].astype(low)
        g[b, :, 128:256] = (grad_q[:, 128:256] + shifted[:, 0:128]).astype(low)
        g[b, :, 256:384] = shifted[:, 128:256].astype(low)
        g[b, :, 384:] = R["dv"][rows].astype(low)
        part = dot(g[b], R["w_qkv"][...].reshape(width, 3 * group_width), 1, 1)
        R["nog"][b] = part.astype(low)
        return carry + jnp.sum(part * R["xhat"][b], axis=0, keepdims=True)

    R["gpart"][0:1] = lax.fori_loop(0, seq_n, settle, jnp.zeros((1, width), f32))

    nog, fold = R["nog"], R["sem_fold"]
    for k in range(seq_n - 1):
        t = seq_n - 1 - k

        @pl.when(z == 0)
        def _():
            remote(nog.at[t], R["up_buf"].at[t], fold.at[0, t], fold.at[1, t], up).start()

        @pl.when(z == seq_n - 1)
        def _():
            remote(nog.at[k], R["down_buf"].at[k], fold.at[2, k], fold.at[3, k], down).start()

    def fold_steps(k, early):
        t = seq_n - 1 - k
        near_up = lower if early else jnp.logical_not(lower)

        @pl.when(jnp.logical_and(near_up, jnp.logical_and(z > 0, z < t)))
        def _():
            buf, total = R["up_buf"], R["up_sum"]
            remote(nog.at[t], buf.at[t], fold.at[0, t], fold.at[1, t], up).wait_recv()
            total[t] = (nog[t].astype(f32) + buf[t].astype(f32)).astype(low)
            remote(total.at[t], buf.at[t], fold.at[0, t], fold.at[1, t], up).start()

        @pl.when(
            jnp.logical_and(jnp.logical_not(near_up), jnp.logical_and(z < seq_n - 1, z > k))
        )
        def _():
            buf, total = R["down_buf"], R["down_sum"]
            remote(nog.at[k], buf.at[k], fold.at[2, k], fold.at[3, k], down).wait_recv()
            total[k] = (nog[k].astype(f32) + buf[k].astype(f32)).astype(low)
            remote(total.at[k], buf.at[k], fold.at[2, k], fold.at[3, k], down).start()

    def qkv_rows(e, carry):
        left = jnp.concatenate([R["n1t"][b, e] for b in range(seq_n)], axis=1)
        R["t_qkv"][e] = dot(left, R["g_s"][...].reshape(length, 3 * group_width)).astype(low)
        return carry

    lax.fori_loop(0, fsdp_n, qkv_rows, 0)
    pair_start("qkv", R["sem_rq"])
    small_start("fsdp", fsdp_n, f, R["gpart"], R["gq"], R["sem_g"].at[0])
    fold_steps(0, True)
    all_first("dn", R["sem_ad"], R["sem_rd"])
    pair_add("qkv", R["sem_rq"])
    for k in range(1, seq_n - 1):
        fold_steps(k, True)
    R["block_out"][...] = (
        R["res_s"][...] + dot(R["gated"][...], R["w_dn"][...].reshape(width, ff), 1, 1)
    ).astype(low)
    for k in range(seq_n - 1):
        fold_steps(k, False)
    all_mid("dn", R["sem_ad"])
    small_wait("fsdp", fsdp_n, f, R["gq"], R["sem_g"].at[0])
    total = R["gq"][0]
    for e in range(1, fsdp_n):
        total = total + R["gq"][e]
    R["gz"][...] = total
    small_start("seq", seq_n, z, R["gz"], R["gzall"], R["sem_g"].at[1])
    all_first("in", R["sem_ai"], R["sem_ri"])
    all_cross("dn", R["sem_ad"])
    all_first("out", R["sem_ao"], R["sem_ro"])
    all_mid("in", R["sem_ai"])
    all_mid("out", R["sem_ao"])
    R["qkv_own"][...] = plane_sum("qkv", R["sem_rq"])
    line_start(R["qkv_all"], R["sem_qa"], R["qkv_own"])
    all_cross("in", R["sem_ai"])
    all_cross("out", R["sem_ao"])
    all_last("dn", R["sem_ad"])


    line_step(R["qkv_all"], R["sem_qa"], 1)
    R["fsum"][...] = nog[z].astype(f32)

    @pl.when(z > 0)
    def _():
        remote(nog.at[z], R["up_buf"].at[z], fold.at[0, z], fold.at[1, z], up).wait_recv()
        R["fsum"][...] += R["up_buf"][z].astype(f32)

    @pl.when(z < seq_n - 1)
    def _():
        remote(nog.at[z], R["down_buf"].at[z], fold.at[2, z], fold.at[3, z], down).wait_recv()
        R["fsum"][...] += R["down_buf"][z].astype(f32)

    scaled_one, inverse_one = norm(R["tokens"][...].astype(f32))
    R["input_grad"][...] = (
        R["rg_s"][...]
        + norm_back_rows(R["fsum"][...], scaled_one, inverse_one, R["gain_s"][0:1])
    ).astype(low)
    line_step(R["qkv_all"], R["sem_qa"], 2)
    all_last("in", R["sem_ai"])
    all_last("out", R["sem_ao"])
    for d in range(3, seq_n):
        line_step(R["qkv_all"], R["sem_qa"], d)

    small_wait("seq", seq_n, z, R["gzall"], R["sem_g"].at[1])
    total = R["gzall"][0]
    for g in range(1, seq_n):
        total = total + R["gzall"][g]
    R["gain_grad"][...] = total
    R["down_grad"][...] = R["a_dn"][4].astype(f32)
    R["in_grad"][...] = R["a_in"][4].astype(f32)
    R["out_grad"][...] = R["a_out"][4].astype(f32)
    for g in range(seq_n):
        for j in range(3):
            at = (j * seq_n + g) * group_width
            R["qkv_grad"][:, at : at + group_width] = R["qkv_all"][
                g, :, j * group_width : (j + 1) * group_width
            ].astype(f32)

    for wait in finish:
        wait()
    line_end(R["tok_all"], R["sem_tok"], R["tokens"])
    line_end(R["qkv_all"], R["sem_qa"], R["qkv_own"])
    for key, sems in (("dn", "sem_ad"), ("in", "sem_ai"), ("out", "sem_ao")):
        all_end(key, R[sems])
    for t in range(seq_n):

        @pl.when(z < t)
        def _():
            remote(nog.at[t], R["up_buf"].at[t], fold.at[0, t], fold.at[1, t], up).wait_send()

        @pl.when(z > t)
        def _():
            remote(nog.at[t], R["down_buf"].at[t], fold.at[2, t], fold.at[3, t], down).wait_send()


def fused(
    tokens,
    positions,
    norm1_gain,
    qkv_weight,
    out_weight,
    norm2_gain,
    in_weight,
    down_weight,
    cotangent,
):
    f32 = jnp.float32
    low = jnp.bfloat16
    seq_n = lax.axis_size("seq")
    fsdp_n = lax.axis_size("fsdp")
    f = lax.axis_index("fsdp")
    _, span, width = tokens.shape
    shard = qkv_weight.shape[0]
    ff = down_weight.shape[0]
    heads = HEADS // seq_n
    group = heads * HEAD_DIM
    chunk = next(c for c in (384, 256, 128, ff) if ff % c == 0)
    half_dim = HEAD_DIM // 2
    frequency = theta ** (-jnp.arange(half_dim, dtype=f32) / half_dim)
    frequency = jnp.tile(frequency, 128 // half_dim)[None]
    gains = lax.dynamic_update_slice(
        jnp.zeros((2, width), low), jnp.stack([norm1_gain, norm2_gain]), (0, f * shard)
    )
    arrays = [
        tokens.reshape(span, width),
        positions,
        gains,
        frequency,
        qkv_weight,
        out_weight,
        in_weight,
        down_weight.T,
        cotangent.reshape(span, width),
    ]
    outs = [
        ((span, width), low),
        ((span, width), low),
        ((shard, 3 * width), f32),
        ((shard, width), f32),
        ((shard, 2 * ff), f32),
        ((shard, ff), f32),
        ((2, width), f32),
    ]
    vmem = pltpu.VMEM
    dma = pltpu.SemaphoreType.DMA
    rows = (seq_n, span)
    columns = {"qkv": 3 * group, "out": width, "in": 2 * ff, "dn": ff}
    scratch = [
        vmem(rows + (width,), low),
        vmem((seq_n,) + positions.shape, jnp.int32),
        vmem((fsdp_n, 2, width), low),
        vmem((shard, 3 * group), low),
    ]
    scratch += [vmem((fsdp_n, shard, c), low) for c in columns.values()]
    scratch += [
        vmem(rows + (width,), f32),
        vmem(rows + (width,), low),
        vmem((seq_n, fsdp_n, shard, span), low),
        vmem(rows + (128,), f32),
        vmem(rows + (128,), f32),
        vmem((heads,) + rows + (256,), low),
        vmem(rows + (256,), low),
        vmem((heads,) + rows + (256,), low),
        vmem(rows + (group,), low),
        vmem((heads,) + rows + (group,), low),
        vmem((heads,) + rows + (seq_n * span,), f32),
    ]
    scratch += [vmem(rows + (group,), low)] * 4 + [vmem((heads,) + rows + (group,), low)]
    scratch += [
        vmem((2, width), f32),
        vmem((span, width), f32),
        vmem((span, width), f32),
        vmem((fsdp_n, shard, span), low),
        vmem((fsdp_n, shard, span), low),
        vmem((span, ff), low),
        vmem((span, 2 * ff), low),
        vmem(rows + (256,), f32),
        vmem((seq_n * span, 256), f32),
        vmem((seq_n * span, group), f32),
        vmem(rows + (3 * group,), low),
        vmem(rows + (width,), low),
    ]
    scratch += [vmem(rows + (width,), low)] * 4
    scratch += [
        vmem((shard, 3 * group), low),
        vmem((seq_n, shard, 3 * group), low),
        vmem((span, width), f32),
        vmem((2, width), f32),
        vmem((fsdp_n, 2, width), f32),
        vmem((2, width), f32),
        vmem((seq_n, 2, width), f32),
    ]
    for c in columns.values():
        scratch += [vmem((fsdp_n, shard, c), low)] + [vmem((fsdp_n // 2, shard, c), low)] * 2
    scratch += [vmem((5, shard, columns[key]), low) for key in ("out", "in", "dn")]
    scratch += [dma((4, seq_n)), dma((2, seq_n)), dma((2, fsdp_n))]
    scratch += [dma((6, 4))] * 4
    scratch += [dma((2, seq_n))] * 2 + [dma((4, seq_n))] * 2
    scratch += [dma((2, 2, max(seq_n, fsdp_n)))]
    scratch += [dma((4, 4))] * 4 + [dma((2, 3))] * 3
    space = pl.BlockSpec(memory_space=pltpu.VMEM)
    block_out, input_grad, qkv_grad, out_grad, in_grad, down_grad, gain_grad = pl.pallas_call(
        functools.partial(fused_kernel, (seq_n, fsdp_n, heads, chunk)),
        out_shape=[jax.ShapeDtypeStruct(s, t) for s, t in outs],
        in_specs=[space] * len(arrays),
        out_specs=[space] * len(outs),
        scratch_shapes=scratch,
        compiler_params=pltpu.CompilerParams(
            collective_id=0, has_side_effects=True, vmem_limit_bytes=67043328
        ),
        name="layer",
    )(*arrays)
    gain_out = lax.dynamic_slice(gain_grad, (0, f * shard), (2, shard))
    return (
        block_out[None],
        input_grad[None],
        qkv_grad,
        out_grad,
        in_grad,
        down_grad.T,
        gain_out[0],
        gain_out[1],
    )


def layer(tokens, positions, norm1_gain, qkv_weight, *others):
    seq_n = lax.axis_size("seq")
    shard = qkv_weight.shape[0]
    group = HEADS // seq_n * HEAD_DIM
    square = lax.axis_size("fsdp") // 2 == 4
    tiles = shard % 32 == 0 and group % shard == 0 and tokens.shape[1] % 128 == 0
    run = fused if square and tiles and tokens.shape[0] == 1 and seq_n % 2 == 0 else local
    return run(tokens, positions, norm1_gain, qkv_weight, *others)


def solution(mesh):
    in_specs = (
        P("fsdp", "seq", None),
        P("fsdp", "seq"),
        P("fsdp"),
        P("fsdp", None),
        P("fsdp", None),
        P("fsdp"),
        P("fsdp", None),
        P(None, "fsdp"),
        P("fsdp", "seq", None),
    )
    out_specs = (
        P("fsdp", "seq", None),
        P("fsdp", "seq", None),
        P("fsdp", None),
        P("fsdp", None),
        P("fsdp", None),
        P(None, "fsdp"),
        P("fsdp"),
        P("fsdp"),
    )
    return jax.shard_map(layer, mesh=mesh, in_specs=in_specs, out_specs=out_specs, check_vma=False)
```

```python
import functools

import jax
import jax.numpy as jnp
import numpy as np
from jax import lax
from jax.experimental import pallas as pl
from jax.experimental.pallas import tpu as pltpu
from jax.sharding import PartitionSpec as P

HEADS = 12
HEAD_DIM = 64
MESH = pl.DeviceIdType.MESH

eps = 1e-05
theta = 160000.0


EXTRA = {"gather": 4, "swap": 3, "spread": 5, "fold": 8, "grad": 11, "reduce": 11}


def exchange_kernel(kinds, seq_n, fsdp_n, *refs):
    f32 = jnp.float32
    count = len(kinds)
    ins = refs[:count]
    outs = refs[count : 2 * count]
    rest = list(refs[2 * count :])
    z = lax.axis_index("seq")
    f = lax.axis_index("fsdp")
    pairs = fsdp_n // 2
    chip = f // 2
    core = f % 2
    partner = chip * 2 + 1 - core
    on_seq = any(kind not in ("spread", "reduce") for kind in kinds)
    on_fsdp = any(kind in ("spread", "grad", "reduce") for kind in kinds)

    barrier = pltpu.get_barrier_semaphore()
    waits = 0
    if on_seq:
        for d in range(1, seq_n):
            pl.semaphore_signal(
                barrier, inc=1, device_id={"seq": (z + d) % seq_n}, device_id_type=MESH
            )
        waits += seq_n - 1
    if on_fsdp:
        for d in range(1, pairs):
            pl.semaphore_signal(
                barrier,
                inc=1,
                device_id={"fsdp": ((chip + d) % pairs) * 2 + core},
                device_id_type=MESH,
            )
        pl.semaphore_signal(barrier, inc=1, device_id={"fsdp": partner}, device_id_type=MESH)
        waits += pairs
    pl.semaphore_wait(barrier, waits)

    def remote(src, dst, send, recv, where):
        return pltpu.make_async_remote_copy(
            src_ref=src,
            dst_ref=dst,
            send_sem=send,
            recv_sem=recv,
            device_id=where,
            device_id_type=MESH,
        )

    groups = {kind: [] for kind in EXTRA}
    for kind, src, dst in zip(kinds, ins, outs):
        groups[kind].append((src, dst, [rest.pop(0) for _ in range(EXTRA[kind])]))
    finish = []
    up = {"seq": lax.rem(z + 1, seq_n)}
    down = {"seq": lax.rem(z + seq_n - 1, seq_n)}
    has_up = z < seq_n - 1
    has_down = z > 0

    def line_start(dst, sems, src):
        up_send, up_recv, down_send, down_recv = sems

        @pl.when(has_up)
        def _():
            remote(src, dst.at[z], up_send.at[0], up_recv.at[1], up).start()

        @pl.when(has_down)
        def _():
            remote(src, dst.at[z], down_send.at[0], down_recv.at[1], down).start()

    def line_step(dst, sems, d):
        up_send, up_recv, down_send, down_recv = sems

        @pl.when(z >= d)
        def _():
            block = dst.at[lax.rem(z + seq_n - d, seq_n)]
            remote(block, block, up_send.at[d], up_recv.at[d], up).wait_recv()
            if d < seq_n - 1:

                @pl.when(has_up)
                def _():
                    remote(block, block, up_send.at[d], up_recv.at[d + 1], up).start()

        @pl.when(z + d < seq_n)
        def _():
            block = dst.at[lax.rem(z + d, seq_n)]
            remote(block, block, down_send.at[d], down_recv.at[d], down).wait_recv()
            if d < seq_n - 1:

                @pl.when(has_down)
                def _():
                    remote(block, block, down_send.at[d], down_recv.at[d + 1], down).start()

    def line_end(dst, sems, src):
        up_send, up_recv, down_send, down_recv = sems
        for d in range(seq_n - 1):

            @pl.when(jnp.logical_and(has_up, z >= d))
            def _():
                block = src if d == 0 else dst.at[lax.rem(z + seq_n - d, seq_n)]
                remote(block, dst.at[z], up_send.at[d], up_recv.at[d + 1], up).wait_send()

            @pl.when(jnp.logical_and(has_down, z + d < seq_n))
            def _():
                block = src if d == 0 else dst.at[lax.rem(z + d, seq_n)]
                remote(block, dst.at[z], down_send.at[d], down_recv.at[d + 1], down).wait_send()

    lower = z * 2 < seq_n

    def fold_steps(k, first):
        t = seq_n - 1 - k
        for src, dst, extra in groups["fold"]:
            up_buf, up_sum, down_buf, down_sum, up_send, up_recv, down_send, down_recv = extra
            near_up = lower if first else jnp.logical_not(lower)

            @pl.when(jnp.logical_and(near_up, jnp.logical_and(z > 0, z < t)))
            def _():
                remote(src.at[t], up_buf.at[t], up_send.at[t], up_recv.at[t], up).wait_recv()
                up_sum[t] = (src[t].astype(f32) + up_buf[t].astype(f32)).astype(src.dtype)
                remote(up_sum.at[t], up_buf.at[t], up_send.at[t], up_recv.at[t], up).start()

            @pl.when(
                jnp.logical_and(
                    jnp.logical_not(near_up), jnp.logical_and(z < seq_n - 1, z > k)
                )
            )
            def _():
                remote(src.at[k], down_buf.at[k], down_send.at[k], down_recv.at[k], down).wait_recv()
                down_sum[k] = (src[k].astype(f32) + down_buf[k].astype(f32)).astype(src.dtype)
                remote(down_sum.at[k], down_buf.at[k], down_send.at[k], down_recv.at[k], down).start()

    for src, dst, extra in groups["grad"] + groups["reduce"]:
        held, total, send_a, recv_a, send_b, recv_b = extra[:6]
        for d in range(pairs):
            block = ((chip + d) % pairs) * 2
            remote(
                src.at[block + 1 - core], held.at[d], send_a.at[d], recv_a.at[d], {"fsdp": partner}
            ).start()
    for src, dst, extra in groups["gather"]:
        line_start(dst, extra, src)
    for k in range(seq_n - 1):
        t = seq_n - 1 - k
        for src, dst, extra in groups["fold"]:
            up_buf, up_sum, down_buf, down_sum, up_send, up_recv, down_send, down_recv = extra

            @pl.when(z == 0)
            def _():
                remote(src.at[t], up_buf.at[t], up_send.at[t], up_recv.at[t], up).start()

            @pl.when(z == seq_n - 1)
            def _():
                remote(src.at[k], down_buf.at[k], down_send.at[k], down_recv.at[k], down).start()

    for src, dst, extra in groups["swap"]:
        send, recv, own = extra
        for d in range(1, seq_n):
            to = (z + d) % seq_n
            piece = src.at[to]
            copy = remote(piece, dst.at[z], send.at[d], recv.at[d], {"seq": to})
            copy.start()
            finish.append(copy.wait_send)
            origin = (z + seq_n - d) % seq_n
            arrival = remote(piece, dst.at[origin], send.at[d], recv.at[d], {"seq": to})
            finish.append(arrival.wait_recv)
        local_copy = pltpu.make_async_copy(src.at[z], dst.at[z], own.at[0])
        local_copy.start()
        finish.append(local_copy.wait)
    for src, dst, extra in groups["spread"]:
        send_a, recv_a, send_b, recv_b, own = extra
        for d in range(1, pairs):
            copy = remote(
                src,
                dst.at[f],
                send_a.at[d],
                recv_a.at[d],
                {"fsdp": ((chip + d) % pairs) * 2 + core},
            )
            copy.start()
            finish.append(copy.wait_send)
        copy = remote(src, dst.at[f], send_b.at[0], recv_b.at[0], {"fsdp": partner})
        copy.start()
        finish.append(copy.wait_send)
        local_copy = pltpu.make_async_copy(src, dst.at[f], own.at[0])
        local_copy.start()
        finish.append(local_copy.wait)
    for src, dst, extra in groups["gather"]:
        dst[z] = src[...]
    for src, dst, extra in groups["grad"] + groups["reduce"]:
        held, total, send_a, recv_a, send_b, recv_b = extra[:6]
        for d in list(range(1, pairs)) + [0]:
            block = ((chip + d) % pairs) * 2
            pair_copy = remote(
                src.at[block + 1 - core], held.at[d], send_a.at[d], recv_a.at[d], {"fsdp": partner}
            )
            pair_copy.wait_recv()
            finish.append(pair_copy.wait_send)
            total[d] = (src[block + core].astype(f32) + held[d].astype(f32)).astype(src.dtype)
            if d > 0:
                copy = remote(
                    total.at[d],
                    extra[10].at[d],
                    send_b.at[d],
                    recv_b.at[d],
                    {"fsdp": block + core},
                )
                copy.start()
                finish.append(copy.wait_send)
    for d in range(1, seq_n):
        for src, dst, extra in groups["gather"]:
            line_step(dst, extra, d)
        for e in range(1, pairs) if d == max(seq_n - 2, 1) else ():
            for src, dst, extra in groups["spread"]:
                send_a, recv_a, send_b, recv_b, own = extra
                origin = ((chip + pairs - e) % pairs) * 2 + core
                remote(src, dst.at[origin], send_a.at[e], recv_a.at[e], {"fsdp": partner}).wait_recv()
                copy = remote(
                    dst.at[origin], dst.at[origin], send_b.at[e], recv_b.at[e], {"fsdp": partner}
                )
                copy.start()
                finish.append(copy.wait_send)
        fold_steps(d - 1, True)
    for k in range(seq_n - 1):
        fold_steps(k, False)

    for j in range(len(groups["grad"]) + seq_n - 1):
        for d in range(1, seq_n):
            if 0 <= j - d < len(groups["grad"]):
                line_step(groups["grad"][j - d][1], groups["grad"][j - d][2][6:10], d)
        if j >= len(groups["grad"]):
            continue
        src, dst, extra = groups["grad"][j]
        held, total, send_a, recv_a, send_b, recv_b = extra[:6]
        value = total[0].astype(f32)
        for d in range(1, pairs):
            remote(
                total.at[d], extra[10].at[d], send_b.at[d], recv_b.at[d], {"fsdp": partner}
            ).wait_recv()
            value = value + extra[10][d].astype(f32)
        dst[z] = value.astype(src.dtype)
        line_start(dst, extra[6:10], dst.at[z])
    for src, dst, extra in groups["reduce"]:
        total, send_b, recv_b = extra[1], extra[4], extra[5]
        value = total[0].astype(f32)
        for d in range(1, pairs):
            remote(
                total.at[d], extra[10].at[d], send_b.at[d], recv_b.at[d], {"fsdp": partner}
            ).wait_recv()
            value = value + extra[10][d].astype(f32)
        dst[...] = value.astype(src.dtype)
    for src, dst, extra in groups["fold"]:
        up_buf, up_sum, down_buf, down_sum, up_send, up_recv, down_send, down_recv = extra
        dst[...] = src[z].astype(f32)

        @pl.when(z > 0)
        def _():
            remote(src.at[z], up_buf.at[z], up_send.at[z], up_recv.at[z], up).wait_recv()
            dst[...] += up_buf[z].astype(f32)

        @pl.when(z < seq_n - 1)
        def _():
            remote(src.at[z], down_buf.at[z], down_send.at[z], down_recv.at[z], down).wait_recv()
            dst[...] += down_buf[z].astype(f32)

        for t in range(seq_n):

            @pl.when(z < t)
            def _():
                remote(src.at[t], up_buf.at[t], up_send.at[t], up_recv.at[t], up).wait_send()

            @pl.when(z > t)
            def _():
                remote(src.at[t], down_buf.at[t], down_send.at[t], down_recv.at[t], down).wait_send()

    for src, dst, extra in groups["spread"]:
        send_a, recv_a, send_b, recv_b, own = extra
        for d in range(pairs):
            origin = ((chip + pairs - d) % pairs) * 2 + 1 - core
            finish.append(
                remote(src, dst.at[origin], send_b.at[d], recv_b.at[d], {"fsdp": partner}).wait_recv
            )
    for wait in finish:
        wait()
    for src, dst, extra in groups["gather"]:
        line_end(dst, extra, src)
    for src, dst, extra in groups["grad"]:
        line_end(dst, extra[6:10], dst.at[z])


def exchange(kinds, arrays, collective_id):
    seq_n = lax.axis_size("seq")
    fsdp_n = lax.axis_size("fsdp")
    pairs = fsdp_n // 2
    results = []
    scratch = []
    dma = pltpu.SemaphoreType.DMA
    for kind, array in zip(kinds, arrays):
        dtype = array.dtype
        if kind == "gather":
            shape = (seq_n,) + array.shape
            scratch += [dma((seq_n,))] * 4
        elif kind == "swap":
            shape = array.shape
            scratch += [dma((seq_n,)), dma((seq_n,)), dma((1,))]
        elif kind == "fold":
            shape = array.shape[1:]
            scratch += [pltpu.VMEM(array.shape, dtype)] * 4 + [dma((seq_n,))] * 4
            dtype = jnp.float32
        elif kind == "spread":
            shape = (fsdp_n,) + array.shape
            scratch += [dma((pairs,))] * 4 + [dma((1,))]
        else:
            shape = array.shape[1:]
            if kind == "grad":
                shape = (seq_n,) + shape
            half = pltpu.VMEM((pairs,) + array.shape[1:], dtype)
            scratch += [half] * 2 + [dma((pairs,))] * 4 + [dma((seq_n,))] * 4 + [half]
        results.append(jax.ShapeDtypeStruct(shape, dtype))
    space = pl.BlockSpec(memory_space=pltpu.VMEM)
    return pl.pallas_call(
        functools.partial(exchange_kernel, tuple(kinds), seq_n, fsdp_n),
        out_shape=results,
        in_specs=[space] * len(kinds),
        out_specs=[space] * len(kinds),
        scratch_shapes=scratch,
        compiler_params=pltpu.CompilerParams(collective_id=collective_id, has_side_effects=True),
        name=f"exchange_{collective_id}",
    )(*arrays)


def layer_norm(values, gain_vec):
    middle = jnp.mean(values, axis=-1, keepdims=True)
    centred = values - middle
    inverse = lax.rsqrt(jnp.mean(centred * centred, axis=-1, keepdims=True) + eps)
    scaled = centred * inverse
    return (scaled * gain_vec, scaled, inverse)


def norm_back(upstream, scaled, inverse, gain_vec):
    weighted = upstream * gain_vec
    return inverse * (
        weighted
        - jnp.mean(weighted, axis=-1, keepdims=True)
        - scaled * jnp.mean(weighted * scaled, axis=-1, keepdims=True)
    )


def rotary_tables(positions, head_size):
    half_dim = head_size // 2
    frequency = theta ** (-jnp.arange(half_dim, dtype=jnp.float32) / half_dim)
    angles = positions.astype(jnp.float32)[..., None] * frequency
    return (jnp.cos(angles), jnp.sin(angles))


def rotate(values, cosine_table, sine_table):
    half_dim = values.shape[-1] // 2
    first_half = values[..., :half_dim]
    second_half = values[..., half_dim:]
    return jnp.concatenate(
        [
            first_half * cosine_table - second_half * sine_table,
            second_half * cosine_table + first_half * sine_table,
        ],
        axis=-1,
    )


def gelu_slope(values):
    return (
        0.5 * (1.0 + lax.erf(values * 0.7071067811865476))
        + values * jnp.exp(-0.5 * values * values) * 0.3989422804014327
    )


def dot(left, right, left_dim=1, right_dim=0):
    return lax.dot_general(
        left, right, (((left_dim,), (right_dim,)), ((), ())), preferred_element_type=jnp.float32
    )


def local(
    tokens,
    positions,
    norm1_gain,
    qkv_weight,
    out_weight,
    norm2_gain,
    in_weight,
    down_weight,
    cotangent,
):
    f32 = jnp.float32
    low = jnp.bfloat16
    groups = lax.axis_size("seq")
    fsdp_n = lax.axis_size("fsdp")
    z = lax.axis_index("seq")
    seq_dev, span_len, width = tokens.shape
    rows = seq_dev * span_len
    length = span_len * groups
    local_heads = HEADS // groups
    group_width = local_heads * HEAD_DIM
    shard = qkv_weight.shape[0]
    ff = down_weight.shape[0]
    ff_part = ff // groups
    scale = HEAD_DIM ** (-0.5)

    def pick(weight, sections, section):
        part = None
        for g in range(groups):
            columns = [
                weight[:, (j * groups + g) * section : (j * groups + g + 1) * section]
                for j in range(sections)
            ]
            own = jnp.concatenate(columns, axis=1)
            part = own if part is None else jnp.where(z == g, own, part)
        return part

    qkv_part = pick(qkv_weight, 3, group_width)
    in_part = pick(in_weight, 2, ff_part)
    down_part = lax.dynamic_slice_in_dim(down_weight, z * ff_part, ff_part, 0).T
    gains = jnp.stack([norm1_gain, norm2_gain])
    own_tokens = tokens.reshape(rows, width)
    own_cotangent = cotangent.reshape(rows, width)

    def whole(stack):
        w = stack.shape[-1]
        return jnp.swapaxes(stack.reshape(groups, seq_dev, span_len, w), 0, 1).reshape(
            seq_dev * length, w
        )

    def spans(full):
        w = full.shape[-1]
        return jnp.swapaxes(full.reshape(seq_dev, groups, span_len, w), 0, 1).reshape(
            groups, rows, w
        )

    all_tokens, all_cot, all_pos, w_qkv, w_out, w_in, w_down, all_gains = exchange(
        ["gather", "gather", "gather", "spread", "spread", "spread", "spread", "spread"],
        [own_tokens, own_cotangent, positions, qkv_part, out_weight, in_part, down_part, gains],
        0,
    )
    all_tokens = whole(all_tokens)
    all_cot = whole(all_cot)
    all_pos = jnp.swapaxes(all_pos, 0, 1).reshape(seq_dev, length)
    w_qkv = w_qkv.reshape(width, 3 * group_width)
    w_out = w_out.reshape(width, width)
    w_in = w_in.reshape(width, 2 * ff_part)
    w_down = w_down.reshape(width, ff_part)
    gain_one = all_gains[:, 0].reshape(width).astype(f32)
    gain_two = all_gains[:, 1].reshape(width).astype(f32)

    normed_one, scaled_full, _ = layer_norm(all_tokens.astype(f32), gain_one)
    normed_one = normed_one.astype(low)
    projected = dot(normed_one, w_qkv).reshape(seq_dev, length, 3, local_heads, HEAD_DIM)
    projected = projected.transpose(2, 0, 3, 1, 4)
    cosine, sine = rotary_tables(all_pos, HEAD_DIM)
    cosine = cosine[:, None]
    sine = sine[:, None]
    query = rotate(projected[0], cosine, sine).astype(low)
    key = rotate(projected[1], cosine, sine).astype(low)
    value = projected[2].astype(low)
    scores = jnp.einsum("bhqd,bhkd->bhqk", query, key, preferred_element_type=f32) * scale
    totals = jax.nn.logsumexp(scores, axis=-1, keepdims=True)
    probs = jnp.exp(scores - totals)
    probs_low = probs.astype(low)
    attended = jnp.einsum("bhqk,bhkd->bhqd", probs_low, value, preferred_element_type=f32).astype(
        low
    )

    def to_rows(heads):
        return jnp.concatenate([heads[:, h] for h in range(local_heads)], axis=-1).reshape(
            seq_dev * length, group_width
        )

    (mixed,) = exchange(["swap"], [spans(to_rows(attended))], 1)
    w_out = w_out.reshape(groups, group_width, width)
    inputs = own_tokens.astype(f32)
    residual = inputs + jnp.einsum("grd,gdw->rw", mixed, w_out, preferred_element_type=f32)
    normed_two, scaled_two, inverse_two = layer_norm(residual, gain_two)
    normed_two = normed_two.astype(low)
    (normed_full,) = exchange(["gather"], [normed_two], 2)
    normed_full = whole(normed_full)
    lifted = dot(normed_full, w_in)
    act = lifted[:, :ff_part]
    gate = lifted[:, ff_part:]
    activated = jax.nn.gelu(act, approximate=False)
    gated = (activated * gate).astype(low)
    gated_grad = dot(all_cot, w_down)
    lifted_grad = jnp.concatenate(
        [gated_grad * gate * gelu_slope(act), gated_grad * activated], axis=1
    ).astype(low)
    ffn_part = dot(gated, w_down, 1, 1).astype(low)
    normed_grad_part = dot(lifted_grad, w_in, 1, 1).astype(low)
    in_term = dot(normed_full, lifted_grad, 0, 0).astype(low)
    down_term = dot(all_cot, gated, 0, 0).astype(low)

    def by_owner(term):
        return term.reshape(fsdp_n, shard, term.shape[1])

    normed_two_grad, in_owned, down_owned = exchange(
        ["fold", "reduce", "reduce"],
        [spans(normed_grad_part), by_owner(in_term), by_owner(down_term)],
        3,
    )
    gain_two_grad = jnp.sum(normed_two_grad * scaled_two, axis=0)
    residual_grad = own_cotangent.astype(f32) + norm_back(
        normed_two_grad, scaled_two, inverse_two, gain_two
    )
    residual_low = residual_grad.astype(low)
    mixed_grad = jnp.einsum("rw,gdw->grd", residual_low, w_out, preferred_element_type=f32)
    out_term = jnp.einsum("grd,rw->gdw", mixed, residual_low, preferred_element_type=f32)
    out_term = out_term.astype(low).reshape(width, width)
    head_grad, out_owned = exchange(
        ["swap", "reduce"], [mixed_grad.astype(low), by_owner(out_term)], 4
    )
    head_grad = whole(head_grad).reshape(seq_dev, length, local_heads, HEAD_DIM)
    head_grad = head_grad.transpose(0, 2, 1, 3)
    delta = jnp.sum(head_grad.astype(f32) * attended.astype(f32), axis=-1, keepdims=True)
    value_grad = jnp.einsum("bhqk,bhqd->bhkd", probs_low, head_grad, preferred_element_type=f32)
    prob_grad = jnp.einsum("bhqd,bhkd->bhqk", head_grad, value, preferred_element_type=f32)
    score_grad = (probs * (prob_grad - delta)).astype(low)
    query_grad = jnp.einsum("bhqk,bhkd->bhqd", score_grad, key, preferred_element_type=f32) * scale
    key_grad = jnp.einsum("bhqk,bhqd->bhkd", score_grad, query, preferred_element_type=f32) * scale
    qkv_grad = jnp.concatenate(
        [
            to_rows(rotate(query_grad.astype(low).astype(f32), cosine, -sine).astype(low)),
            to_rows(rotate(key_grad.astype(low).astype(f32), cosine, -sine).astype(low)),
            to_rows(value_grad.astype(low)),
        ],
        axis=1,
    )
    normed_one_grad_part = dot(qkv_grad, w_qkv, 1, 1)
    gain_one_grad = jnp.sum(normed_one_grad_part * scaled_full, axis=0)

    qkv_term = dot(normed_one, qkv_grad, 0, 0).astype(low)
    gain_terms = jnp.stack(
        [gain_one_grad.reshape(fsdp_n, shard), gain_two_grad.reshape(fsdp_n, shard)], axis=1
    )
    parts = exchange(
        ["fold", "fold", "gather", "gather", "gather", "grad", "grad"],
        [spans(normed_one_grad_part.astype(low)), spans(ffn_part)]
        + [in_owned, down_owned, out_owned, by_owner(qkv_term), gain_terms],
        5,
    )
    normed_one_grad = parts[0]
    _, scaled_one, inverse_one = layer_norm(inputs, gain_one)
    input_grad = (
        residual_grad + norm_back(normed_one_grad, scaled_one, inverse_one, gain_one)
    ).astype(low)
    block_out = (residual + parts[1]).astype(low)
    in_all, down_all, out_all, qkv_all, gain_all = parts[2:]

    def columns_of(stack, sections, section):
        return jnp.concatenate(
            [
                stack[g][:, j * section : (j + 1) * section]
                for j in range(sections)
                for g in range(groups)
            ],
            axis=1,
        ).astype(f32)

    qkv_out = columns_of(qkv_all, 3, group_width)
    in_out = columns_of(in_all, 2, ff_part)
    down_out = down_all.transpose(0, 2, 1).reshape(ff, shard).astype(f32)
    out_out = jnp.sum(out_all.astype(f32), axis=0)
    gain_out = jnp.sum(gain_all, axis=0)
    return (
        block_out.reshape(seq_dev, span_len, width),
        input_grad.reshape(seq_dev, span_len, width),
        qkv_out,
        out_out,
        in_out,
        down_out,
        gain_out[0],
        gain_out[1],
    )


def fused_kernel(dims, *refs):
    seq_n, fsdp_n, heads, chunk = dims
    f32 = jnp.float32
    low = jnp.bfloat16
    (
        r_tokens, r_pos, r_gain1, r_gain2, r_freq, r_qkv, r_out, r_inw, r_down, r_cot,
        r_block_out, r_input_grad, r_qkv_grad, r_out_grad, r_in_grad, r_down_grad,
        r_gain1_grad, r_gain2_grad, r_tok_all, r_pos_all, r_gain_src, r_gains_all, r_qkv_src,
        r_w_qkv, r_w_out, r_w_in, r_w_dn, r_xhat, r_n1, r_n1t, r_cosine, r_sine, r_q_m, r_k_s,
        r_k_m, r_v_s, r_v_m, r_p_s, r_att, r_mixed, r_mgrad, r_hgrad, r_hg_m, r_gain_s, r_rg_s,
        r_res_s, r_n2t, r_cott, r_gated, r_lifted_grad, r_dq, r_dk, r_dv, r_g_s, r_nog,
        r_up_buf, r_up_sum, r_down_buf, r_down_sum, r_qkv_own, r_qkv_all, r_fsum, r_gpart,
        r_gq, r_gz, r_gzall, r_t_qkv, r_h_qkv, r_r_qkv, r_t_out, r_h_out, r_r_out, r_t_ia,
        r_h_ia, r_r_ia, r_t_ib, r_h_ib, r_r_ib, r_t_dn, r_h_dn, r_r_dn, r_a_out, r_a_ia,
        r_a_ib, r_a_dn, r_sem_tok, r_sem_pos, r_sem_gain, r_sem_wq, r_sem_wo, r_sem_wi,
        r_sem_wd, r_sem_sw1, r_sem_sw2, r_sem_fold, r_sem_qa, r_sem_g, r_sem_rq, r_sem_ro,
        r_sem_ria, r_sem_rib, r_sem_rd, r_sem_ao, r_sem_aia, r_sem_aib, r_sem_ad,
    ) = refs
    t_qkv = (r_t_qkv, r_h_qkv, r_r_qkv, r_sem_rq)
    t_out = (r_t_out, r_h_out, r_r_out, r_sem_ro, r_a_out, r_sem_ao)
    t_ia = (r_t_ia, r_h_ia, r_r_ia, r_sem_ria, r_a_ia, r_sem_aia)
    t_ib = (r_t_ib, r_h_ib, r_r_ib, r_sem_rib, r_a_ib, r_sem_aib)
    t_dn = (r_t_dn, r_h_dn, r_r_dn, r_sem_rd, r_a_dn, r_sem_ad)
    z = lax.axis_index("seq")
    f = lax.axis_index("fsdp")
    chip = f // 2
    core = f % 2
    px = chip % 2
    py = chip // 2
    flip = [chip, py * 2 + 1 - px, (1 - py) * 2 + px, (1 - py) * 2 + 1 - px]
    partner = {"fsdp": chip * 2 + 1 - core}
    span, width = r_tokens.shape
    shard = r_out.shape[0]
    group_width = r_att.shape[2]
    head_dim = group_width // heads
    half_dim = head_dim // 2
    ff = r_down.shape[1]
    scale = head_dim ** (-0.5)
    half = shard // 2

    barrier = pltpu.get_barrier_semaphore()
    for d in range(1, seq_n):
        pl.semaphore_signal(
            barrier, inc=1, device_id={"seq": (z + d) % seq_n}, device_id_type=MESH
        )
    for d in range(1, fsdp_n):
        pl.semaphore_signal(
            barrier, inc=1, device_id={"fsdp": (f + d) % fsdp_n}, device_id_type=MESH
        )
    pl.semaphore_wait(barrier, seq_n + fsdp_n - 2)

    finish = []

    def remote(src, dst, send, recv, where):
        return pltpu.make_async_remote_copy(
            src_ref=src,
            dst_ref=dst,
            send_sem=send,
            recv_sem=recv,
            device_id=where,
            device_id_type=MESH,
        )

    def send(src, dst, send_sem, recv_sem, where):
        copy = remote(src, dst, send_sem, recv_sem, where)
        copy.start()
        finish.append(copy.wait_send)

    def await_recv(dst, send_sem, recv_sem, where):
        remote(dst, dst, send_sem, recv_sem, where).wait_recv()

    up = {"seq": lax.rem(z + 1, seq_n)}
    down = {"seq": lax.rem(z + seq_n - 1, seq_n)}
    has_up = z < seq_n - 1
    has_down = z > 0

    def small_start(axis, count, me, src, dst, sems):
        dst[me] = src[...]
        for d in range(1, count):
            send(src, dst.at[me], sems.at[0, d], sems.at[1, d], {axis: (me + d) % count})

    def small_wait(axis, count, me, dst, sems):
        for d in range(1, count):
            origin = (me + count - d) % count
            await_recv(dst.at[origin], sems.at[0, d], sems.at[1, d], {axis: origin})

    def line_start(dst, sems, src):
        dst[z] = src[...]

        @pl.when(has_up)
        def _():
            remote(src, dst.at[z], sems.at[0, 0], sems.at[1, 1], up).start()

        @pl.when(has_down)
        def _():
            remote(src, dst.at[z], sems.at[2, 0], sems.at[3, 1], down).start()

    def line_step(dst, sems, d):
        @pl.when(z >= d)
        def _():
            block = dst.at[lax.rem(z + seq_n - d, seq_n)]
            remote(block, block, sems.at[0, d], sems.at[1, d], up).wait_recv()
            if d < seq_n - 1:

                @pl.when(has_up)
                def _():
                    remote(block, block, sems.at[0, d], sems.at[1, d + 1], up).start()

        @pl.when(z + d < seq_n)
        def _():
            block = dst.at[lax.rem(z + d, seq_n)]
            remote(block, block, sems.at[2, d], sems.at[3, d], down).wait_recv()
            if d < seq_n - 1:

                @pl.when(has_down)
                def _():
                    remote(block, block, sems.at[2, d], sems.at[3, d + 1], down).start()

    def line_end(dst, sems, src):
        for d in range(seq_n - 1):

            @pl.when(jnp.logical_and(has_up, z >= d))
            def _():
                block = src if d == 0 else dst.at[lax.rem(z + seq_n - d, seq_n)]
                remote(block, dst.at[z], sems.at[0, d], sems.at[1, d + 1], up).wait_send()

            @pl.when(jnp.logical_and(has_down, z + d < seq_n))
            def _():
                block = src if d == 0 else dst.at[lax.rem(z + d, seq_n)]
                remote(block, dst.at[z], sems.at[2, d], sems.at[3, d + 1], down).wait_send()

    def spread_start(src, dst, sems):
        for nb in (1, 2):
            send(src, dst.at[f], sems.at[0, nb], sems.at[1, nb], {"fsdp": flip[nb] * 2 + core})
        send(src, dst.at[f], sems.at[2, 0], sems.at[3, 0], partner)
        dst[f] = src[...]

    def spread_one(dst, sems):
        for nb in (1, 2):
            origin = flip[nb] * 2 + core
            await_recv(dst.at[origin], sems.at[0, nb], sems.at[1, nb], partner)
            part = dst.at[origin, pl.ds((nb - 1) * half, half)]
            send(part, part, sems.at[4, nb], sems.at[5, nb], {"fsdp": flip[3 - nb] * 2 + core})
            send(dst.at[origin], dst.at[origin], sems.at[2, nb], sems.at[3, nb], partner)

    def spread_two(dst, sems):
        origin = flip[3] * 2 + core
        for nb in (1, 2):
            part = dst.at[origin, pl.ds((nb - 1) * half, half)]
            await_recv(part, sems.at[4, nb], sems.at[5, nb], partner)
        send(dst.at[origin], dst.at[origin], sems.at[2, 3], sems.at[3, 3], partner)

    def spread_wait(dst, sems):
        for e in range(4):
            origin = flip[e] * 2 + 1 - core
            await_recv(dst.at[origin], sems.at[2, e], sems.at[3, e], partner)

    def swap_start(src, dst, sems):
        for d in range(1, seq_n):
            to = (z + d) % seq_n
            send(src.at[to], dst.at[z], sems.at[0, d], sems.at[1, d], {"seq": to})
        dst[z] = src[z]

    def swap_wait(dst, sems):
        for d in range(1, seq_n):
            origin = (z + seq_n - d) % seq_n
            await_recv(dst.at[origin], sems.at[0, d], sems.at[1, d], {"seq": origin})

    def pair_start(term):
        src, held, _, sems = term[:4]
        for d in (3, 1, 2, 0):
            send(src.at[flip[d] * 2 + 1 - core], held.at[d], sems.at[0, d], sems.at[1, d], partner)

    sides = [pl.ds(0, half), pl.ds(half, half)]

    def pair_add(term):
        src, held, got, sems = term[:4]
        for d in (3, 1, 2, 0):
            await_recv(held.at[d], sems.at[0, d], sems.at[1, d], partner)
            held[d] = (src[flip[d] * 2 + core].astype(f32) + held[d].astype(f32)).astype(low)
            for h in range(2):
                if d == 3 or d == 1 + h:
                    slot = 1 if d == 3 else 0
                    send(
                        held.at[d, sides[h]],
                        got.at[slot, sides[h]],
                        sems.at[2, slot * 2 + h],
                        sems.at[3, slot * 2 + h],
                        {"fsdp": flip[1 + h] * 2 + core},
                    )

    def pair_relay(term):
        _, held, got, sems = term[:4]
        for h in range(2):
            await_recv(got.at[1, sides[h]], sems.at[2, 2 + h], sems.at[3, 2 + h], partner)
            d = 2 - h
            held[d, sides[h]] = (
                held[d, sides[h]].astype(f32) + got[1, sides[h]].astype(f32)
            ).astype(low)
            send(
                held.at[d, sides[h]],
                got.at[2, sides[h]],
                sems.at[2, 4 + h],
                sems.at[3, 4 + h],
                {"fsdp": flip[d] * 2 + core},
            )

    def plane_sum(term, h):
        _, held, got, sems = term[:4]
        await_recv(got.at[0, sides[h]], sems.at[2, h], sems.at[3, h], partner)
        await_recv(got.at[2, sides[h]], sems.at[2, 4 + h], sems.at[3, 4 + h], partner)
        return (
            held[0, sides[h]].astype(f32)
            + got[0, sides[h]].astype(f32)
            + got[2, sides[h]].astype(f32)
        ).astype(low)

    mid = seq_n // 2
    lower = z < mid
    depth = jnp.where(lower, z, seq_n - 1 - z)
    inner = {"seq": jnp.where(lower, z + 1, z - 1)}
    outer = {"seq": jnp.where(lower, lax.rem(z + seq_n - 1, seq_n), lax.rem(z + 1, seq_n))}

    def all_first(term, h):
        buf, sems = term[4].at[:, sides[h]], term[5].at[h]
        buf[0] = plane_sum(term, h)

        @pl.when(depth == 0)
        def _():
            remote(buf.at[0], buf.at[1], sems.at[0, 0], sems.at[1, 0], inner).start()

    def all_mid(term, h):
        buf, sems = term[4].at[:, sides[h]], term[5].at[h]

        @pl.when(depth > 0)
        def _():
            remote(buf.at[1], buf.at[1], sems.at[0, 0], sems.at[1, 0], outer).wait_recv()
            buf[2] = (buf[0].astype(f32) + buf[1].astype(f32)).astype(low)

            @pl.when(depth < mid - 1)
            def _():
                remote(buf.at[2], buf.at[1], sems.at[0, 0], sems.at[1, 0], inner).start()

            @pl.when(depth == mid - 1)
            def _():
                remote(buf.at[2], buf.at[3], sems.at[0, 1], sems.at[1, 1], inner).start()

    def all_cross(term, h):
        buf, sems = term[4].at[:, sides[h]], term[5].at[h]

        @pl.when(depth == mid - 1)
        def _():
            remote(buf.at[3], buf.at[3], sems.at[0, 1], sems.at[1, 1], inner).wait_recv()
            buf[4] = (buf[2].astype(f32) + buf[3].astype(f32)).astype(low)
            remote(buf.at[4], buf.at[4], sems.at[0, 2], sems.at[1, 2], outer).start()

    def all_last(term, h):
        buf, sems = term[4].at[:, sides[h]], term[5].at[h]

        @pl.when(depth < mid - 1)
        def _():
            remote(buf.at[4], buf.at[4], sems.at[0, 2], sems.at[1, 2], inner).wait_recv()

            @pl.when(depth > 0)
            def _():
                remote(buf.at[4], buf.at[4], sems.at[0, 2], sems.at[1, 2], outer).start()

    def all_end(term, h):
        buf, sems = term[4].at[:, sides[h]], term[5].at[h]

        @pl.when(depth == 0)
        def _():
            remote(buf.at[0], buf.at[1], sems.at[0, 0], sems.at[1, 0], inner).wait_send()

        @pl.when(depth > 0)
        def _():
            @pl.when(depth < mid - 1)
            def _():
                remote(buf.at[2], buf.at[1], sems.at[0, 0], sems.at[1, 0], inner).wait_send()

            @pl.when(depth == mid - 1)
            def _():
                remote(buf.at[2], buf.at[3], sems.at[0, 1], sems.at[1, 1], inner).wait_send()

            remote(buf.at[4], buf.at[4], sems.at[0, 2], sems.at[1, 2], outer).wait_send()

    small_start("seq", seq_n, z, r_pos, r_pos_all, r_sem_pos)
    r_gain_src[0:1] = r_gain1[...].astype(f32)
    r_gain_src[1:2] = r_gain2[...].astype(f32)
    small_start("fsdp", fsdp_n, f, r_gain_src, r_gains_all, r_sem_gain)
    line_start(r_tok_all, r_sem_tok, r_tokens)
    for g in range(seq_n):

        @pl.when(z == g)
        def _():
            for j in range(3):
                at = (j * seq_n + g) * group_width
                r_qkv_src[:, j * group_width : (j + 1) * group_width] = r_qkv[
                    :, at : at + group_width
                ]

    spread_start(r_qkv_src, r_w_qkv, r_sem_wq)
    spread_start(r_out, r_w_out, r_sem_wo)

    lane = lax.broadcasted_iota(jnp.int32, (1, 128), 1)
    first = lax.rem(lane, head_dim) < half_dim

    def turn(values, rows, sign):
        pieces = []
        for c in range(values.shape[1] // 128):
            u = values[:, c * 128 : (c + 1) * 128]
            w = jnp.where(
                first, pltpu.roll(u, 128 - half_dim, 1), pltpu.roll(u, half_dim, 1)
            )
            pieces.append(u * r_cosine[rows] + sign * (w * r_sine[rows]))
        return jnp.concatenate(pieces, axis=1)

    wide = lax.broadcasted_iota(jnp.int32, (1, 256), 1)

    def masked(values, h):
        at = lax.broadcasted_iota(jnp.int32, values.shape, 1)
        keep = jnp.logical_and(at >= h * head_dim, at < (h + 1) * head_dim)
        return jnp.where(keep, values, 0.0).astype(low)

    def norm(values):
        centred = values - jnp.mean(values, axis=-1, keepdims=True)
        inverse = lax.rsqrt(jnp.mean(centred * centred, axis=-1, keepdims=True) + eps)
        return centred * inverse, inverse

    def norm_block(b):
        scaled, _ = norm(r_tok_all[b].astype(f32))
        r_xhat[b] = scaled
        normed = (scaled * r_gain_s[0:1]).astype(low)
        r_n1[b] = normed
        r_n1t[b] = normed.astype(f32).T.astype(low).reshape(fsdp_n, shard, span)

    def project_block(b):
        got = dot(r_n1[b], r_w_qkv[...].reshape(width, 3 * group_width))
        row = r_pos_all[b].astype(f32)
        angle = jnp.broadcast_to(row, (128, span)).T * r_freq[...]
        r_cosine[b] = jnp.cos(angle)
        sine = jnp.sin(angle)
        r_sine[b] = jnp.where(first, -sine, sine)
        q = turn(got[:, 0:256], b, 1.0).astype(low).astype(f32)
        k = turn(pltpu.roll(got[:, 128:512], 384 - 64, 1)[:, 0:256], b, 1.0).astype(low)
        k = jnp.where(wide < group_width, k.astype(f32), 0.0)
        v = got[:, 2 * group_width :].astype(low).astype(f32)
        r_k_s[b] = k.astype(low)
        r_v_s[b] = v.astype(low)
        for h in range(heads):
            r_q_m[h, b] = masked(q, h)
            r_k_m[h, b] = masked(k, h)
            r_v_m[h, b] = masked(v, h)

    spread_one(r_w_qkv, r_sem_wq)
    spread_start(r_inw, r_w_in, r_sem_wi)
    small_wait("seq", seq_n, z, r_pos_all, r_sem_pos)
    small_wait("fsdp", fsdp_n, f, r_gains_all, r_sem_gain)
    for e in range(fsdp_n):
        r_gain_s[:, e * shard : (e + 1) * shard] = r_gains_all[e]
    norm_block(z)
    line_step(r_tok_all, r_sem_tok, 1)
    spread_one(r_w_out, r_sem_wo)
    spread_start(r_down, r_w_dn, r_sem_wd)
    spread_two(r_w_qkv, r_sem_wq)
    spread_wait(r_w_qkv, r_sem_wq)
    project_block(z)
    for d in range(1, seq_n):
        if d > 1:
            line_step(r_tok_all, r_sem_tok, d)

        def arrived(side, carry):
            block = jnp.where(side == 0, z - d, z + d)

            @pl.when(jnp.logical_and(block >= 0, block < seq_n))
            def _():
                b = lax.rem(block + seq_n, seq_n)
                norm_block(b)
                project_block(b)

            return carry

        lax.fori_loop(0, 2, arrived, 0)

    length = span * seq_n

    def forward_rows(b, carry):
        result = None
        for h in range(heads):
            scores = dot(r_q_m[h, b], r_k_s[...].reshape(length, 256), 1, 1) * scale
            top = jnp.max(scores, axis=-1, keepdims=True)
            exps = jnp.exp(scores - top)
            probs = exps / jnp.sum(exps, axis=-1, keepdims=True)
            r_p_s[h, b] = probs
            piece = dot(probs.astype(low), r_v_m[h].reshape(length, group_width))
            result = piece if result is None else result + piece
        r_att[b] = result.astype(low)
        return carry

    lax.fori_loop(0, seq_n, forward_rows, 0)
    swap_start(r_att, r_mixed, r_sem_sw1)
    spread_one(r_w_in, r_sem_wi)
    spread_two(r_w_out, r_sem_wo)
    spread_wait(r_w_out, r_sem_wo)
    cot = r_cot[...]
    r_cott[...] = cot.astype(f32).T.astype(low).reshape(fsdp_n, shard, span)
    spread_one(r_w_dn, r_sem_wd)

    swap_wait(r_mixed, r_sem_sw1)
    w_out = r_w_out[...].reshape(width, width)
    residual = r_tokens[...].astype(f32)
    for g in range(seq_n):
        residual = residual + dot(
            r_mixed[g], w_out[g * group_width : (g + 1) * group_width]
        )
    r_res_s[...] = residual
    scaled_two, inverse_two = norm(residual)
    normed_two = (scaled_two * r_gain_s[1:2]).astype(low)
    r_n2t[...] = normed_two.astype(f32).T.astype(low).reshape(fsdp_n, shard, span)
    spread_two(r_w_in, r_sem_wi)
    spread_wait(r_w_in, r_sem_wi)
    spread_two(r_w_dn, r_sem_wd)
    spread_wait(r_w_dn, r_sem_wd)

    for c in range(0, ff, chunk):
        a = dot(normed_two, r_w_in[:, :, c : c + chunk].reshape(width, chunk))
        g = dot(normed_two, r_w_in[:, :, ff + c : ff + c + chunk].reshape(width, chunk))
        gg = dot(cot, r_w_dn[:, :, c : c + chunk].reshape(width, chunk))
        cdf = 0.5 * (1.0 + lax.erf(a * 0.7071067811865476))
        activated = a * cdf
        slope = cdf + a * jnp.exp(-0.5 * a * a) * 0.3989422804014327
        r_gated[:, c : c + chunk] = (activated * g).astype(low)
        r_lifted_grad[:, c : c + chunk] = (gg * g * slope).astype(low)
        r_lifted_grad[:, ff + c : ff + c + chunk] = (gg * activated).astype(low)
    def down_rows(e, carry):
        r_t_dn[e] = dot(r_cott[e], r_gated[...]).astype(low)
        return carry

    lax.fori_loop(0, fsdp_n, down_rows, 0)
    pair_start(t_dn)

    lifted_grad = r_lifted_grad[...]
    gated = r_gated[...]
    normed_two_grad = dot(lifted_grad, r_w_in[...].reshape(width, 2 * ff), 1, 1)
    r_gpart[1:2] = jnp.sum(normed_two_grad * scaled_two, axis=0, keepdims=True)

    def norm_back_rows(upstream, scaled, inverse, gain_vec):
        weighted = upstream * gain_vec
        return inverse * (
            weighted
            - jnp.mean(weighted, axis=-1, keepdims=True)
            - scaled * jnp.mean(weighted * scaled, axis=-1, keepdims=True)
        )

    residual_grad = cot.astype(f32) + norm_back_rows(
        normed_two_grad, scaled_two, inverse_two, r_gain_s[1:2]
    )
    r_rg_s[...] = residual_grad
    residual_low = residual_grad.astype(low)
    for g in range(seq_n):
        r_mgrad[g] = dot(
            residual_low, w_out[g * group_width : (g + 1) * group_width], 1, 1
        ).astype(low)
    swap_start(r_mgrad, r_hgrad, r_sem_sw2)

    pair_add(t_dn)

    def in_rows(e, carry):
        r_t_ia[e] = dot(r_n2t[e], r_lifted_grad[:, 0:ff]).astype(low)
        return carry

    lax.fori_loop(0, fsdp_n, in_rows, 0)
    pair_start(t_ia)

    def gate_rows(e, carry):
        r_t_ib[e] = dot(r_n2t[e], r_lifted_grad[:, ff:]).astype(low)
        return carry

    lax.fori_loop(0, fsdp_n, gate_rows, 0)
    pair_start(t_ib)
    own = group_width // shard
    for g in range(seq_n):
        r_t_out[g * own : (g + 1) * own] = (
            dot(r_mixed[g], residual_low, 0, 0).astype(low).reshape(own, shard, width)
        )
    pair_start(t_out)

    swap_wait(r_hgrad, r_sem_sw2)
    for h in range(heads):
        for b in range(seq_n):
            r_hg_m[h, b] = masked(r_hgrad[b].astype(f32), h)
    r_dk[...] = jnp.zeros(r_dk.shape, f32)
    r_dv[...] = jnp.zeros(r_dv.shape, f32)

    def backward_rows(b, carry):
        grad_q = None
        attended = r_att[b].astype(f32)
        for h in range(heads):
            probs = r_p_s[h, b]
            upstream = r_hg_m[h, b]
            delta = jnp.sum(upstream.astype(f32) * attended, axis=-1, keepdims=True)
            prob_grad = dot(upstream, r_v_s[...].reshape(length, group_width), 1, 1)
            score_grad = (probs * (prob_grad - delta)).astype(low)
            piece = dot(score_grad, r_k_m[h].reshape(length, 256))
            grad_q = piece if grad_q is None else grad_q + piece
            r_dk[...] += dot(score_grad, r_q_m[h, b], 0, 0)
            r_dv[...] += dot(probs.astype(low), upstream, 0, 0)
        r_dq[b] = grad_q
        return carry

    lax.fori_loop(0, seq_n // 2, backward_rows, 0)
    pair_add(t_ia)
    lax.fori_loop(seq_n // 2, seq_n, backward_rows, 0)
    pair_relay(t_dn)

    def settle(b, carry):
        rows = pl.ds(pl.multiple_of(b * span, span), span)
        grad_q = turn((r_dq[b] * scale).astype(low).astype(f32), b, -1.0)
        grad_k = turn((r_dk[rows] * scale).astype(low).astype(f32), b, -1.0)
        shifted = pltpu.roll(grad_k, 64, 1)
        g = r_g_s
        g[b, :, 0:128] = grad_q[:, 0:128].astype(low)
        g[b, :, 128:256] = (grad_q[:, 128:256] + shifted[:, 0:128]).astype(low)
        g[b, :, 256:384] = shifted[:, 128:256].astype(low)
        g[b, :, 384:] = r_dv[rows].astype(low)
        part = dot(g[b], r_w_qkv[...].reshape(width, 3 * group_width), 1, 1)
        r_nog[b] = part.astype(low)
        return carry + jnp.sum(part * r_xhat[b], axis=0, keepdims=True)

    r_gpart[0:1] = lax.fori_loop(0, seq_n, settle, jnp.zeros((1, width), f32))

    nog, fold = r_nog, r_sem_fold
    for k in range(seq_n - 1):
        t = seq_n - 1 - k

        @pl.when(z == 0)
        def _():
            remote(nog.at[t], r_up_buf.at[t], fold.at[0, t], fold.at[1, t], up).start()

        @pl.when(z == seq_n - 1)
        def _():
            remote(nog.at[k], r_down_buf.at[k], fold.at[2, k], fold.at[3, k], down).start()

    def fold_steps(k, early):
        t = seq_n - 1 - k
        near_up = lower if early else jnp.logical_not(lower)

        @pl.when(jnp.logical_and(near_up, jnp.logical_and(z > 0, z < t)))
        def _():
            buf, total = r_up_buf, r_up_sum
            remote(nog.at[t], buf.at[t], fold.at[0, t], fold.at[1, t], up).wait_recv()
            total[t] = (nog[t].astype(f32) + buf[t].astype(f32)).astype(low)
            remote(total.at[t], buf.at[t], fold.at[0, t], fold.at[1, t], up).start()

        @pl.when(
            jnp.logical_and(jnp.logical_not(near_up), jnp.logical_and(z < seq_n - 1, z > k))
        )
        def _():
            buf, total = r_down_buf, r_down_sum
            remote(nog.at[k], buf.at[k], fold.at[2, k], fold.at[3, k], down).wait_recv()
            total[k] = (nog[k].astype(f32) + buf[k].astype(f32)).astype(low)
            remote(total.at[k], buf.at[k], fold.at[2, k], fold.at[3, k], down).start()

    def qkv_rows(e, carry):
        left = jnp.concatenate([r_n1t[b, e] for b in range(seq_n)], axis=1)
        r_t_qkv[e] = dot(left, r_g_s[...].reshape(length, 3 * group_width)).astype(low)
        return carry

    lax.fori_loop(0, fsdp_n, qkv_rows, 0)
    pair_start(t_qkv)
    small_start("fsdp", fsdp_n, f, r_gpart, r_gq, r_sem_g.at[0])
    pair_add(t_ib)
    pair_relay(t_ia)
    pair_add(t_qkv)
    fold_steps(0, True)
    all_first(t_dn, 0)
    all_first(t_dn, 1)
    r_block_out[...] = (
        r_res_s[...] + dot(r_gated[...], r_w_dn[...].reshape(width, ff), 1, 1)
    ).astype(low)
    pair_relay(t_ib)
    pair_add(t_out)
    for k in range(1, seq_n - 1):
        fold_steps(k, True)
    for k in range(seq_n - 1):
        fold_steps(k, False)
    all_mid(t_dn, 0)
    all_mid(t_dn, 1)
    all_first(t_ia, 0)
    all_first(t_ia, 1)
    pair_relay(t_qkv)
    all_cross(t_dn, 0)
    all_cross(t_dn, 1)
    pair_relay(t_out)
    r_fsum[...] = nog[z].astype(f32)

    @pl.when(z > 0)
    def _():
        remote(nog.at[z], r_up_buf.at[z], fold.at[0, z], fold.at[1, z], up).wait_recv()
        r_fsum[...] += r_up_buf[z].astype(f32)

    @pl.when(z < seq_n - 1)
    def _():
        remote(nog.at[z], r_down_buf.at[z], fold.at[2, z], fold.at[3, z], down).wait_recv()
        r_fsum[...] += r_down_buf[z].astype(f32)

    scaled_one, inverse_one = norm(r_tokens[...].astype(f32))
    r_input_grad[...] = (
        r_rg_s[...]
        + norm_back_rows(r_fsum[...], scaled_one, inverse_one, r_gain_s[0:1])
    ).astype(low)
    for h in range(2):
        r_qkv_own[sides[h]] = plane_sum(t_qkv, h)
    line_start(r_qkv_all, r_sem_qa, r_qkv_own)
    all_mid(t_ia, 0)
    all_mid(t_ia, 1)
    all_first(t_ib, 0)
    all_first(t_ib, 1)
    all_last(t_dn, 0)
    all_last(t_dn, 1)
    small_wait("fsdp", fsdp_n, f, r_gq, r_sem_g.at[0])
    total = r_gq[0]
    for e in range(1, fsdp_n):
        total = total + r_gq[e]
    r_gz[...] = total
    small_start("seq", seq_n, z, r_gz, r_gzall, r_sem_g.at[1])
    all_cross(t_ia, 0)
    all_cross(t_ia, 1)
    all_mid(t_ib, 0)
    all_mid(t_ib, 1)
    line_step(r_qkv_all, r_sem_qa, 1)
    all_first(t_out, 0)
    all_first(t_out, 1)
    all_last(t_ia, 0)
    all_last(t_ia, 1)
    all_cross(t_ib, 0)
    all_cross(t_ib, 1)
    all_mid(t_out, 0)
    all_mid(t_out, 1)
    for d in range(2, seq_n):
        line_step(r_qkv_all, r_sem_qa, d)
    all_cross(t_out, 0)
    all_cross(t_out, 1)
    all_last(t_ib, 0)
    all_last(t_ib, 1)
    small_wait("seq", seq_n, z, r_gzall, r_sem_g.at[1])
    total = r_gzall[0]
    for g in range(1, seq_n):
        total = total + r_gzall[g]
    for e in range(fsdp_n):

        @pl.when(f == e)
        def _():
            r_gain1_grad[...] = total[0:1, e * shard : (e + 1) * shard]
            r_gain2_grad[...] = total[1:2, e * shard : (e + 1) * shard]

    for g in range(seq_n):
        for j in range(3):
            at = (j * seq_n + g) * group_width
            r_qkv_grad[:, at : at + group_width] = r_qkv_all[
                g, :, j * group_width : (j + 1) * group_width
            ]
    r_down_grad[...] = r_a_dn[4]
    r_in_grad[:, 0:ff] = r_a_ia[4]
    r_in_grad[:, ff:] = r_a_ib[4]
    all_last(t_out, 0)
    all_last(t_out, 1)
    r_out_grad[...] = r_a_out[4]

    for wait in finish:
        wait()
    line_end(r_tok_all, r_sem_tok, r_tokens)
    line_end(r_qkv_all, r_sem_qa, r_qkv_own)
    for term in (t_dn, t_ia, t_ib, t_out):
        for h in range(2):
            all_end(term, h)
    for t in range(seq_n):

        @pl.when(z < t)
        def _():
            remote(nog.at[t], r_up_buf.at[t], fold.at[0, t], fold.at[1, t], up).wait_send()

        @pl.when(z > t)
        def _():
            remote(nog.at[t], r_down_buf.at[t], fold.at[2, t], fold.at[3, t], down).wait_send()


def fused(
    tokens,
    positions,
    norm1_gain,
    qkv_weight,
    out_weight,
    norm2_gain,
    in_weight,
    down_weight,
    cotangent,
):
    f32 = jnp.float32
    low = jnp.bfloat16
    seq_n = lax.axis_size("seq")
    fsdp_n = lax.axis_size("fsdp")
    _, span, width = tokens.shape
    shard = qkv_weight.shape[0]
    ff = down_weight.shape[0]
    heads = HEADS // seq_n
    group = heads * HEAD_DIM
    chunk = next(c for c in (384, 256, 128, ff) if ff % c == 0)
    half_dim = HEAD_DIM // 2
    frequency = theta ** (-np.arange(half_dim) / half_dim)
    frequency = jnp.asarray(np.tile(frequency, 128 // half_dim)[None], f32)
    arrays = [
        tokens.reshape(span, width),
        positions,
        norm1_gain[None],
        norm2_gain[None],
        frequency,
        qkv_weight,
        out_weight,
        in_weight,
        down_weight.T,
        cotangent.reshape(span, width),
    ]
    outs = [
        ((span, width), low),
        ((span, width), low),
        ((shard, 3 * width), low),
        ((shard, width), low),
        ((shard, 2 * ff), low),
        ((shard, ff), low),
        ((1, shard), f32),
        ((1, shard), f32),
    ]
    vmem = pltpu.VMEM
    dma = pltpu.SemaphoreType.DMA
    rows = (seq_n, span)
    columns = (3 * group, width, 2 * ff, ff)
    pieces = (3 * group, width, ff, ff, ff)
    scratch = [
        vmem(rows + (width,), low),
        vmem((seq_n,) + positions.shape, jnp.int32),
        vmem((2, shard), f32),
        vmem((fsdp_n, 2, shard), f32),
        vmem((shard, 3 * group), low),
    ]
    scratch += [vmem((fsdp_n, shard, c), low) for c in columns]
    scratch += [
        vmem(rows + (width,), f32),
        vmem(rows + (width,), low),
        vmem((seq_n, fsdp_n, shard, span), low),
        vmem(rows + (128,), f32),
        vmem(rows + (128,), f32),
        vmem((heads,) + rows + (256,), low),
        vmem(rows + (256,), low),
        vmem((heads,) + rows + (256,), low),
        vmem(rows + (group,), low),
        vmem((heads,) + rows + (group,), low),
        vmem((heads,) + rows + (seq_n * span,), f32),
    ]
    scratch += [vmem(rows + (group,), low)] * 4 + [vmem((heads,) + rows + (group,), low)]
    scratch += [
        vmem((2, width), f32),
        vmem((span, width), f32),
        vmem((span, width), f32),
        vmem((fsdp_n, shard, span), low),
        vmem((fsdp_n, shard, span), low),
        vmem((span, ff), low),
        vmem((span, 2 * ff), low),
        vmem(rows + (256,), f32),
        vmem((seq_n * span, 256), f32),
        vmem((seq_n * span, group), f32),
        vmem(rows + (3 * group,), low),
        vmem(rows + (width,), low),
    ]
    scratch += [vmem(rows + (width,), low)] * 4
    scratch += [
        vmem((shard, 3 * group), low),
        vmem((seq_n, shard, 3 * group), low),
        vmem((span, width), f32),
        vmem((2, width), f32),
        vmem((fsdp_n, 2, width), f32),
        vmem((2, width), f32),
        vmem((seq_n, 2, width), f32),
    ]
    for c in pieces:
        scratch += [vmem((fsdp_n, shard, c), low)] + [vmem((fsdp_n // 2, shard, c), low)] * 2
    scratch += [vmem((5, shard, c), low) for c in pieces[1:]]
    scratch += [dma((4, seq_n)), dma((2, seq_n)), dma((2, fsdp_n))]
    scratch += [dma((6, 4))] * 4
    scratch += [dma((2, seq_n))] * 2 + [dma((4, seq_n))] * 2
    scratch += [dma((2, 2, max(seq_n, fsdp_n)))]
    scratch += [dma((4, 6))] * 5 + [dma((2, 2, 3))] * 4
    space = pl.BlockSpec(memory_space=pltpu.VMEM)
    results = pl.pallas_call(
        functools.partial(fused_kernel, (seq_n, fsdp_n, heads, chunk)),
        out_shape=[jax.ShapeDtypeStruct(s, t) for s, t in outs],
        in_specs=[space] * len(arrays),
        out_specs=[space] * len(outs),
        scratch_shapes=scratch,
        compiler_params=pltpu.CompilerParams(
            collective_id=0, has_side_effects=True, vmem_limit_bytes=67043328
        ),
        name="layer",
    )(*arrays)
    block_out, input_grad, qkv_grad, out_grad, in_grad, down_grad, gain1, gain2 = results
    return (
        block_out[None],
        input_grad[None],
        qkv_grad.astype(f32),
        out_grad.astype(f32),
        in_grad.astype(f32),
        down_grad.T.astype(f32),
        gain1[0],
        gain2[0],
    )


def layer(tokens, positions, norm1_gain, qkv_weight, *others):
    seq_n = lax.axis_size("seq")
    shard = qkv_weight.shape[0]
    group = HEADS // seq_n * HEAD_DIM
    square = lax.axis_size("fsdp") // 2 == 4
    tiles = shard % 32 == 0 and group % shard == 0 and tokens.shape[1] % 128 == 0
    run = fused if square and tiles and tokens.shape[0] == 1 and seq_n % 2 == 0 else local
    return run(tokens, positions, norm1_gain, qkv_weight, *others)


def solution(mesh):
    in_specs = (
        P("fsdp", "seq", None),
        P("fsdp", "seq"),
        P("fsdp"),
        P("fsdp", None),
        P("fsdp", None),
        P("fsdp"),
        P("fsdp", None),
        P(None, "fsdp"),
        P("fsdp", "seq", None),
    )
    out_specs = (
        P("fsdp", "seq", None),
        P("fsdp", "seq", None),
        P("fsdp", None),
        P("fsdp", None),
        P("fsdp", None),
        P(None, "fsdp"),
        P("fsdp"),
        P("fsdp"),
    )
    return jax.shard_map(layer, mesh=mesh, in_specs=in_specs, out_specs=out_specs, check_vma=False)
```
